32 devices in a mesh: gx: 4 (over z), gy: 4 (over y, x), gz: 2 (over core).
Axes of the slice: x: 2, y: 2, z: 4, core: 2. Of those that a mesh axis runs over, the one named last changes fastest.
Arguments:
- phi: bfloat16 [64, 128, 8, 512], P('gx', None, 'gy', 'gz'), may hold values from -6 to 6
- pot: float32 [64, 8, 512], P('gx', 'gy', 'gz'), may hold values from -1 to 1
- kern: bfloat16 [64, 16, 128, 128], P('gx'), may hold values from -0.06982422 to 0.06982422
- kern_hk: bfloat16 [64, 16, 128, 128], P('gx'), may hold values from -0.119628906 to 0.119628906
- slot_of: int32 [64, 16], P('gx'), may hold values from 0 to 31, as said below
- req_cols: int32 [128], P('gx'), may hold values from 0 to 63, as said below
Outputs:
- grad: bfloat16 [64, 128, 8, 512], P('gx', None, 'gy', 'gz')
The draws below stay inside these ranges and needn't reach their ends.
Inputs may be any that keep to these rules, and one draw needn't show every extreme that they name: `slot_of`: each row's entries are distinct. `req_cols`: the 32 entries of group d are distinct, name columns of exactly 2 groups (d itself among them), exactly 16 of each, listed by increasing owning group; column c belongs to group c // 16.
All inputs are finite; a program needn't handle non-finite values.
Results may differ from the reference program's by a relative error of at most 0.011.
Values may be sent and summed in bfloat16 or wider, within the bound.
No kernel may reach another device: no remote copies, remote signals or barrier semaphores. Data moves between devices by JAX's collectives and lax.ppermute only.
A program may use at most 192 MiB of HBM per device.

```python
import jax
import jax.numpy as jnp
from jax import lax

B = 128
NB = 16
NNZ = 16
NU = 32
PY = 8
PZ = 512
NBTOT = 64
OWNERS = 2
CAP = 16
N_GX = 4


def draw_req_cols(key, part):
    group_count = NBTOT // NB

    def one_group(group):
        group_key = jax.random.fold_in(key, group)
        pick_key = jax.random.fold_in(group_key, 11)
        rows_key = jax.random.fold_in(group_key, 23)
        others = jax.random.permutation(pick_key, group_count - 1)[:OWNERS - 1]
        others = jnp.where(others >= group, others + 1, others)
        chosen = jnp.zeros((group_count,), jnp.int32).at[group].set(1).at[others].set(1)
        owners = jnp.nonzero(chosen, size=OWNERS)[0].astype(jnp.int32)

        def rows_of(owner):
            return jax.random.permutation(jax.random.fold_in(rows_key, owner), NB)[:CAP].astype(jnp.int32)
        picked = jax.vmap(rows_of)(owners)
        return (owners[:, None] * NB + picked).reshape(-1)
    return jax.vmap(one_group)(jnp.arange(group_count, dtype=jnp.int32)).reshape(-1).astype(jnp.int32)


def draw_slot_of(key, part):

    def one_row(row):
        return jax.random.permutation(jax.random.fold_in(key, row), NU)[:NNZ].astype(jnp.int32)
    return jax.vmap(one_row)(jnp.arange(NBTOT, dtype=jnp.int32)).astype(jnp.int32)


def levels(stream_key, shape, cuts, smallest, high):
    loudness = 1.0
    for axis_at, blocks in cuts:
        draws = jax.random.uniform(jax.random.fold_in(jax.random.fold_in(stream_key, 6), axis_at), (blocks,), jnp.float32, smallest / len(cuts), high / len(cuts))
        loudness = loudness * jnp.repeat(jnp.exp(draws), shape[axis_at] // blocks).reshape((-1,) + (1,) * (len(shape) - 1 - axis_at))
    return loudness


def noise(key, dims, deviation, most, split=(), held_as=jnp.bfloat16):
    result = deviation * jax.random.normal(key, dims, jnp.float32)
    if split:
        result = result * levels(key, dims, split, -0.22, 0.18)
    return jnp.clip(result, -most, most).astype(held_as)


def setup_inputs(seed: int = 0) -> dict:
    keys = jax.random.split(jax.random.key(seed), 7)
    return {
        "phi": noise(keys[0], (NBTOT, B, PY, PZ), 1.0, 6.0, ((0, 4), (2, 4), (3, 2))),
        "pot": jnp.clip(jax.random.uniform(keys[1], (NBTOT, PY, PZ), jnp.float32, -1.0, 1.0) * levels(keys[1], (NBTOT, PY, PZ), ((0, 4), (1, 4), (2, 2)), -0.4, 0.0), -1.0, 1.0),
        "kern": noise(keys[2], (NBTOT, NNZ, B, B), 0.012, 0.06982422, ((0, 4),)),
        "kern_hk": noise(keys[3], (NBTOT, NNZ, B, B), 0.02, 0.119628906, ((0, 4),)),
        "slot_of": draw_slot_of(jax.random.fold_in(keys[6], 71), 0),
        "req_cols": draw_req_cols(jax.random.fold_in(keys[6], 71), 0),
    }


def hamiltonian_action(phi, pot):
    field = phi.astype(jnp.float32)
    padded = jnp.pad(field, ((0, 0), (0, 0), (1, 1), (1, 1)))
    beside_all = padded[:, :, 2:, 1:-1] + padded[:, :, :-2, 1:-1] + padded[:, :, 1:-1, 2:] + padded[:, :, 1:-1, :-2]
    return (-0.5 * (beside_all - 4.0 * field) + pot[:, None, :, :] * field).astype(jnp.bfloat16)


def reference(phi, pot, kern, kern_hk, slot_of, req_cols):
    action = hamiltonian_action(phi, pot)
    blocks = B
    rows_y = PY
    rows_z = PZ

    def one_group(group):
        first = (group * NB).astype(jnp.int32)
        kern_g = lax.dynamic_slice_in_dim(kern, first, NB, 0).astype(jnp.float32)
        hk_g = lax.dynamic_slice_in_dim(kern_hk, first, NB, 0).astype(jnp.float32)
        act_g = lax.dynamic_slice_in_dim(action, first, NB, 0).astype(jnp.float32)
        phi_g = lax.dynamic_slice_in_dim(phi, first, NB, 0).astype(jnp.float32)
        slots = lax.dynamic_slice_in_dim(slot_of, first, NB, 0).reshape(-1)
        terms = jnp.einsum("ikab,iayz->ikbyz", kern_g, act_g) - jnp.einsum("ikab,iayz->ikbyz", hk_g, phi_g)
        terms = terms.reshape(NB * NNZ, blocks, rows_y, rows_z)
        summed = jnp.zeros((NU, blocks, rows_y, rows_z), jnp.float32).at[slots].add(terms)
        return summed.astype(jnp.bfloat16)

    partial_value = lax.map(one_group, jnp.arange(N_GX, dtype=jnp.int32))
    flat = partial_value.reshape(N_GX * NU, blocks, rows_y, rows_z).astype(jnp.float32)
    total = jnp.zeros((NBTOT, blocks, rows_y, rows_z), jnp.float32).at[req_cols].add(flat)
    return (2.0 * total).astype(jnp.bfloat16)
```

```python
import functools

import jax
import jax.numpy as jnp
import numpy as np
from jax import lax
from jax.experimental import pallas as pl
from jax.experimental.pallas import tpu as pltpu
from jax.sharding import PartitionSpec as P

CHUNKS = 2
LANES = 128
MIB = 1 << 20


def regroup_matrix(block, parts):
    rows = np.arange(block * parts)
    out = np.zeros((block * parts, block * parts), np.float32)
    out[rows, (rows % parts) * block + rows // parts] = 1.0
    return jnp.asarray(out, jnp.bfloat16)


def prepare_kernel(per_step, chunks, rows_y, tiles, phi_ref, mix_ref, *out_refs):
    block = mix_ref.shape[0]
    size = block // (tiles * rows_y)
    zc = tiles * LANES // chunks
    for step in range(per_step):
        part = phi_ref[step * block : (step + 1) * block, :]
        turned = lax.dot_general(
            part, mix_ref[...], (((0,), (0,)), ((), ())), preferred_element_type=jnp.float32
        ).astype(jnp.bfloat16)
        for chunk in range(chunks):
            tile, low = divmod(chunk * zc, LANES)
            for y in range(rows_y):
                at = (tile * rows_y + y) * size
                for more in range(max(1, zc // LANES)):
                    lane = at + more * rows_y * size
                    rows = min(zc, LANES)
                    out_refs[chunk * rows_y + y][step, more * LANES : more * LANES + rows, :] = turned[
                        low : low + rows, lane : lane + size
                    ]


def prepare(phi, chunks):
    groups, block, rows_y, rows_z = phi.shape
    tiles = rows_z // LANES
    flat = (
        phi.reshape(groups, block, rows_y, tiles, LANES)
        .transpose(0, 1, 3, 2, 4)
        .reshape(groups * block * tiles * rows_y, LANES)
    )
    parts = tiles * rows_y
    zc = rows_z // chunks
    per_step = 4
    outs = pl.pallas_call(
        functools.partial(prepare_kernel, per_step, chunks, rows_y, tiles),
        grid=(groups // per_step,),
        in_specs=[
            pl.BlockSpec((per_step * block * parts, LANES), lambda s: (s, 0)),
            pl.BlockSpec((block * parts, block * parts), lambda s: (0, 0)),
        ],
        out_specs=[pl.BlockSpec((per_step, zc, block), lambda s: (s, 0, 0))] * (chunks * rows_y),
        out_shape=[jax.ShapeDtypeStruct((groups, zc, block), jnp.bfloat16)] * (chunks * rows_y),
        name="prepare",
    )(flat, regroup_matrix(block, parts))
    return [[outs[c * rows_y + y] for y in range(rows_y)] for c in range(chunks)]


def gather_kernel(cols, groups, which_ref, kern_ref, hk_ref, out_ref, zero_ref, sem):
    zero_ref[...] = jnp.zeros_like(zero_ref)

    @pl.loop(0, cols)
    def _(col):
        for row in range(groups):
            at = which_ref[col * groups + row]

            @pl.when(at >= 0)
            def _():
                pltpu.make_async_copy(kern_ref.at[row, at], out_ref.at[col, row, 0], sem).start()
                pltpu.make_async_copy(hk_ref.at[row, at], out_ref.at[col, row, 1], sem).start()

            @pl.when(at < 0)
            def _():
                pltpu.make_async_copy(zero_ref, out_ref.at[col, row, 0], sem).start()
                pltpu.make_async_copy(zero_ref, out_ref.at[col, row, 1], sem).start()

    pltpu.make_async_copy(out_ref, out_ref, sem).wait()


def gather_blocks(kern, kern_hk, which):
    cols, groups = which.shape
    block = kern.shape[-1]
    shape = (cols, groups, 2, block, block)
    return pl.pallas_call(
        functools.partial(gather_kernel, cols, groups),
        grid_spec=pltpu.PrefetchScalarGridSpec(
            num_scalar_prefetch=1,
            grid=(1,),
            in_specs=[pl.BlockSpec(memory_space=pl.ANY)] * 2,
            out_specs=pl.BlockSpec(memory_space=pl.ANY),
            scratch_shapes=[pltpu.VMEM((block, block), jnp.bfloat16), pltpu.SemaphoreType.DMA(())],
        ),
        out_shape=jax.ShapeDtypeStruct(shape, jnp.bfloat16),
        cost_estimate=pl.CostEstimate(flops=0, transcendentals=0, bytes_accessed=4 * int(np.prod(shape))),
        name="gather_blocks",
    )(which.reshape(-1), kern, kern_hk)


def fill_operand(groups, rows_y, x_ref, y_refs, prev_ref, next_ref, low_ref, high_ref, pot_ref):
    zc, block = y_refs[0].shape[1:]
    z = lax.broadcasted_iota(jnp.int32, (zc, block), 0)
    for row in range(groups):
        fields = [ref[row].astype(jnp.float32) for ref in y_refs]
        above = [prev_ref[row].astype(jnp.float32)] + fields[:-1]
        below = fields[1:] + [next_ref[row].astype(jnp.float32)]
        for y, field in enumerate(fields):
            low = low_ref[y, row : row + 1, :].astype(jnp.float32)
            high = high_ref[y, row : row + 1, :].astype(jnp.float32)
            left = jnp.where(z == 0, low, pltpu.roll(field, 1, 0))
            right = jnp.where(z == zc - 1, high, pltpu.roll(field, zc - 1, 0))
            beside = below[y] + above[y] + right + left
            pot = pot_ref[y * zc : (y + 1) * zc, row : row + 1]
            action = -0.5 * (beside - 4.0 * field) + pot * field
            x_ref[y * zc : (y + 1) * zc, row * 2 * block : row * 2 * block + block] = action.astype(jnp.bfloat16)
            x_ref[y * zc : (y + 1) * zc, row * 2 * block + block : (row + 1) * 2 * block] = -y_refs[y][row]


def columns_of(x, w_ref):
    pair = [w_ref[j].reshape(-1, w_ref.shape[-1]) for j in range(2)]
    return jnp.dot(x, jnp.concatenate(pair, axis=1), preferred_element_type=jnp.float32)


def store_pair(out_ref, value):
    block = out_ref.shape[-1]
    for j in range(2):
        out_ref[j] = value[:, j * block : (j + 1) * block].astype(jnp.bfloat16)


def first_kernel(groups, rows_y, split, *refs):
    y_refs = refs[:rows_y]
    prev_ref, next_ref, low_ref, high_ref, pot_ref, w_ref, x_ref = refs[rows_y : rows_y + 7]
    outs = refs[rows_y + 7 :]
    pair = pl.program_id(0)

    @pl.when(pair == 0)
    def _():
        fill_operand(groups, rows_y, x_ref, y_refs, prev_ref, next_ref, low_ref, high_ref, pot_ref)

    value = columns_of(x_ref[...], w_ref)
    if len(outs) == 1:
        store_pair(outs[0], value)
    else:

        @pl.when(pair < split)
        def _():
            store_pair(outs[0], value)

        @pl.when(pair >= split)
        def _():
            store_pair(outs[1], value)


def first_columns(fields, prev, after, low, high, pot, blocks, halves):
    rows_y = len(fields)
    groups, zc, block = fields[0].shape
    cols = blocks.shape[0]
    pairs = cols // 2
    n = rows_y * zc
    depth = groups * 2 * block
    whole = lambda *shape: pl.BlockSpec(shape, lambda p: (0,) * len(shape))
    split = pairs // 2
    if halves == 2:
        out_specs = [
            pl.BlockSpec((2, n, block), lambda p: (jnp.minimum(p, split - 1), 0, 0)),
            pl.BlockSpec((2, n, block), lambda p: (jnp.maximum(p - split, 0), 0, 0)),
        ]
    else:
        out_specs = [pl.BlockSpec((2, n, block), lambda p: (p, 0, 0))]
    return pl.pallas_call(
        functools.partial(first_kernel, groups, rows_y, split),
        grid=(pairs,),
        in_specs=[whole(groups, zc, block)] * (rows_y + 2)
        + [whole(rows_y, groups, block)] * 2
        + [whole(n, groups), pl.BlockSpec((2, groups, 2, block, block), lambda p: (p, 0, 0, 0, 0))],
        out_specs=[whole(n, depth)] + out_specs,
        out_shape=[jax.ShapeDtypeStruct((n, depth), jnp.bfloat16)]
        + [jax.ShapeDtypeStruct((cols // halves, n, block), jnp.bfloat16)] * halves,
        compiler_params=pltpu.CompilerParams(vmem_limit_bytes=40 * MIB),
        cost_estimate=pl.CostEstimate(
            flops=2 * n * depth * cols * block, transcendentals=0, bytes_accessed=2 * depth * cols * block
        ),
        name="first_columns",
    )(*fields, prev, after, low, high, pot, blocks)


def local_kernel(chunks, *refs):
    x_refs, w_ref, out_refs = refs[:chunks], refs[chunks], refs[chunks + 1 :]
    for x_ref, out_ref in zip(x_refs, out_refs):
        store_pair(out_ref, columns_of(x_ref[...], w_ref))


def local_columns(xs, blocks):
    cols, groups, _, block, _ = blocks.shape
    n, depth = xs[0].shape
    return pl.pallas_call(
        functools.partial(local_kernel, len(xs)),
        grid=(cols // 2,),
        in_specs=[pl.BlockSpec((n, depth), lambda p: (0, 0))] * len(xs)
        + [pl.BlockSpec((2, groups, 2, block, block), lambda p: (p, 0, 0, 0, 0))],
        out_specs=[pl.BlockSpec((2, n, block), lambda p: (p, 0, 0))] * len(xs),
        out_shape=[jax.ShapeDtypeStruct((cols, n, block), jnp.bfloat16)] * len(xs),
        compiler_params=pltpu.CompilerParams(vmem_limit_bytes=40 * MIB),
        cost_estimate=pl.CostEstimate(
            flops=2 * n * len(xs) * depth * cols * block, transcendentals=0, bytes_accessed=2 * depth * cols * block
        ),
        name="local_columns",
    )(*xs, blocks)


def write_columns(rows_y, tiles, values, mix_ref, out_ref, at):
    chunks = len(values)
    zc = values[0].shape[0] // rows_y
    parts = []
    for tile in range(tiles):
        for y in range(rows_y):
            pieces = []
            for chunk in range(chunks):
                first, last = chunk * zc, (chunk + 1) * zc
                lo, hi = max(first, tile * LANES), min(last, (tile + 1) * LANES)
                if lo < hi:
                    pieces.append(values[chunk][y * zc + lo - first : y * zc + hi - first, :])
            parts.append(jnp.concatenate(pieces, axis=0) if len(pieces) > 1 else pieces[0])
    turned = jnp.concatenate([(2.0 * part).astype(jnp.bfloat16) for part in parts], axis=1)
    rows = mix_ref.shape[0]
    out_ref[at * rows : (at + 1) * rows, :] = lax.dot_general(
        mix_ref[...], turned, (((1,), (1,)), ((), ())), preferred_element_type=jnp.float32
    ).astype(jnp.bfloat16)


def final_kernel(per_step, chunks, rows_y, tiles, flags_ref, mix_ref, *refs):
    own, right2, left1, left2, right1 = (refs[k * chunks : (k + 1) * chunks] for k in range(5))
    out_ref = refs[5 * chunks]
    step = pl.program_id(0)
    half = pl.num_programs(0) // 2

    def emit(added, maybe, flag):
        for col in range(per_step):
            values = []
            for chunk in range(chunks):
                extra = jnp.where(flag == 1, maybe[chunk][col].astype(jnp.float32), 0.0)
                values.append(
                    own[chunk][col].astype(jnp.float32) + added[chunk][col].astype(jnp.float32) + extra
                )
            write_columns(rows_y, tiles, values, mix_ref, out_ref, col)

    @pl.when(step < half)
    def _():
        emit(right2, left1, flags_ref[0])

    @pl.when(step >= half)
    def _():
        emit(left2, right1, flags_ref[1])


def finish(flags, own, right2, left1, left2, right1, rows_y, rows_z):
    chunks = len(own)
    cols, n, block = own[0].shape
    tiles = rows_z // LANES
    rows = block * tiles * rows_y
    per_step = 2
    steps = cols // per_step
    half = steps // 2
    all_cols = pl.BlockSpec((per_step, n, block), lambda s, f: (s, 0, 0))
    low_cols = pl.BlockSpec((per_step, n, block), lambda s, f: (jnp.minimum(s, half - 1), 0, 0))
    high_cols = pl.BlockSpec((per_step, n, block), lambda s, f: (jnp.maximum(s - half, 0), 0, 0))
    flat = pl.pallas_call(
        functools.partial(final_kernel, per_step, chunks, rows_y, tiles),
        grid_spec=pltpu.PrefetchScalarGridSpec(
            num_scalar_prefetch=1,
            grid=(steps,),
            in_specs=[pl.BlockSpec((rows, rows), lambda s, f: (0, 0))]
            + [all_cols] * chunks
            + [low_cols] * (2 * chunks)
            + [high_cols] * (2 * chunks),
            out_specs=pl.BlockSpec((per_step * rows, LANES), lambda s, f: (s, 0)),
        ),
        out_shape=jax.ShapeDtypeStruct((cols * rows, LANES), jnp.bfloat16),
        name="finish",
    )(flags, regroup_matrix(block, tiles * rows_y), *own, *right2, *left1, *left2, *right1)
    return unflatten(flat, cols, block, rows_y, tiles)


def unflatten(flat, cols, block, rows_y, tiles):
    return (
        flat.reshape(cols, block, tiles, rows_y, LANES)
        .transpose(0, 1, 3, 2, 4)
        .reshape(cols, block, rows_y, tiles * LANES)
    )


def plain_kernel(per_step, chunks, rows_y, tiles, mix_ref, *refs):
    for col in range(per_step):
        values = [refs[chunk][col].astype(jnp.float32) for chunk in range(chunks)]
        write_columns(rows_y, tiles, values, mix_ref, refs[chunks], col)


def finish_plain(totals, rows_y, rows_z):
    chunks = len(totals)
    cols, n, block = totals[0].shape
    tiles = rows_z // LANES
    rows = block * tiles * rows_y
    per_step = 2
    flat = pl.pallas_call(
        functools.partial(plain_kernel, per_step, chunks, rows_y, tiles),
        grid=(cols // per_step,),
        in_specs=[pl.BlockSpec((rows, rows), lambda s: (0, 0))]
        + [pl.BlockSpec((per_step, n, block), lambda s: (s, 0, 0))] * chunks,
        out_specs=pl.BlockSpec((per_step * rows, LANES), lambda s: (s, 0)),
        out_shape=jax.ShapeDtypeStruct((cols * rows, LANES), jnp.bfloat16),
        name="finish",
    )(regroup_matrix(block, tiles * rows_y), *totals)
    return unflatten(flat, cols, block, rows_y, tiles)


def block_of_column(slot_of, slots):
    hit = slot_of[None, :, :] == slots[:, None, None]
    index = jnp.arange(1, slot_of.shape[1] + 1, dtype=jnp.int32)
    return jnp.sum(jnp.where(hit, index, 0), axis=2) - 1


def shifts(axis, by):
    count = lax.axis_size(axis)
    return [(i, i + by) for i in range(count) if 0 <= i + by < count]


def per_device(phi, pot, kern, kern_hk, slot_of, req_cols):
    groups, block, rows_y, rows_z = phi.shape
    listed = req_cols.shape[0]
    ring = lax.axis_size("gx")
    chunks = CHUNKS
    zc = rows_z // chunks

    fields = prepare(phi, chunks)
    edge_low = jnp.stack([fields[0][y][:, 0, :] for y in range(rows_y)])
    edge_high = jnp.stack([fields[-1][y][:, -1, :] for y in range(rows_y)])
    from_low = lax.ppermute(edge_high, "gz", shifts("gz", 1))
    from_high = lax.ppermute(edge_low, "gz", shifts("gz", -1))
    halo = [
        (
            lax.ppermute(fields[c][-1], "gy", shifts("gy", 1)),
            lax.ppermute(fields[c][0], "gy", shifts("gy", -1)),
        )
        for c in range(chunks)
    ]
    lows = [from_low] + [
        jnp.stack([fields[c - 1][y][:, -1, :] for y in range(rows_y)]) for c in range(1, chunks)
    ]
    highs = [
        jnp.stack([fields[c + 1][y][:, 0, :] for y in range(rows_y)]) for c in range(chunks - 1)
    ] + [from_high]
    pots = [
        pot[:, :, c * zc : (c + 1) * zc].reshape(groups, rows_y * zc).T for c in range(chunks)
    ]

    if ring != 4:
        which = block_of_column(slot_of, jnp.arange(listed, dtype=jnp.int32))
        blocks = gather_blocks(kern, kern_hk, which)
        hit = req_cols[None, :] == jnp.arange(groups * ring, dtype=jnp.int32)[:, None]
        named = jnp.any(hit, axis=1)
        source = jnp.sum(jnp.where(hit, jnp.arange(listed, dtype=jnp.int32), 0), axis=1)
        totals = []
        for c in range(chunks):
            _, part = first_columns(fields[c], *halo[c], lows[c], highs[c], pots[c], blocks, 1)
            spread = jnp.where(named[:, None, None], part[source], 0)
            totals.append(lax.psum_scatter(spread, "gx", scatter_dimension=0, tiled=True))
        return finish_plain(totals, rows_y, rows_z)

    me = lax.axis_index("gx")
    owners = req_cols // groups
    other = jnp.where(owners[0] == me, owners[listed - 1], owners[0])
    away = (other - me) % ring
    ahead = [(i, (i + 1) % ring) for i in range(ring)]
    behind = [(i, (i - 1) % ring) for i in range(ring)]
    left_away = lax.ppermute(away.reshape(1), "gx", ahead)[0]
    right_away = lax.ppermute(away.reshape(1), "gx", behind)[0]

    half = groups // 2
    column = jnp.arange(groups, dtype=jnp.int32)
    swapped = jnp.where(away == 2, column, (column + half) % groups)
    wanted = jnp.concatenate([other * groups + swapped, me * groups + column])
    slots = jnp.sum(
        jnp.where(wanted[:, None] == req_cols[None, :], jnp.arange(listed, dtype=jnp.int32), 0), axis=1
    )
    which = block_of_column(slot_of, slots)
    far_blocks = gather_blocks(kern, kern_hk, which[:groups])
    near_blocks = gather_blocks(kern, kern_hk, which[groups:])

    xs, sent, right1, left1, right2, left2 = [], [], [], [], [], []
    for c in range(chunks):
        x, q0, q1 = first_columns(fields[c], *halo[c], lows[c], highs[c], pots[c], far_blocks, 2)
        xs.append(x)
        sent.append((q0, q1))
        right1.append(lax.ppermute(q0, "gx", ahead))
        left1.append(lax.ppermute(q1, "gx", behind))
    own = local_columns(xs, near_blocks)
    for c in range(chunks):
        q0, q1 = sent[c]

        def onward(mine, is_mine, arrived, is_through):
            kept = jnp.where(is_mine, mine.astype(jnp.float32), 0.0)
            through = jnp.where(is_through, arrived.astype(jnp.float32), 0.0)
            return (kept + through).astype(jnp.bfloat16)

        right2.append(lax.ppermute(onward(q1, away == 1, right1[c], left_away == 2), "gx", ahead))
        left2.append(lax.ppermute(onward(q0, away == ring - 1, left1[c], right_away == 2), "gx", behind))
    flags = jnp.stack([right_away == ring - 1, left_away == 1]).astype(jnp.int32)
    return finish(flags, own, right2, left1, left2, right1, rows_y, rows_z)


def solution(mesh):
    placed = (
        P("gx", None, "gy", "gz"),
        P("gx", "gy", "gz"),
        P("gx", None, None, None),
        P("gx", None, None, None),
        P("gx", None),
        P("gx"),
    )
    return jax.shard_map(
        per_device, mesh=mesh, in_specs=placed, out_specs=P("gx", None, "gy", "gz"), check_vma=False
    )
```

```python
import functools

import jax
import jax.numpy as jnp
import numpy as np
from jax import lax
from jax.experimental import pallas as pl
from jax.experimental.pallas import tpu as pltpu
from jax.sharding import PartitionSpec as P

CUTS = (0, 128, 256)
RIGHT, ACROSS, LEFT = 1, 2, 3
LANES = 128
SCOPED = 14 << 20
VMEM = pl.BlockSpec(memory_space=pltpu.VMEM)


def in_hbm(*arrays):
    return [pltpu.with_memory_space_constraint(array, pltpu.HBM) for array in arrays]


def after(value, *before):
    return lax.optimization_barrier((value, *before))[0]


def regroup_matrix(block, parts):
    rows = np.arange(block * parts)
    out = np.zeros((block * parts, block * parts), np.float32)
    out[rows, (rows % parts) * block + rows // parts] = 1.0
    return jnp.asarray(out, jnp.bfloat16)


def stencil_matrix(zc, rows_y):
    out = np.zeros((rows_y, zc, rows_y + 2, zc), np.float32)
    z = np.arange(zc)
    for y in range(rows_y):
        out[y, z, y, z] = 0.5
        out[y, z, y + 2, z] = 0.5
        out[y, z, y + 1, z] = -2.0
        out[y, z[1:], y + 1, z[:-1]] = 0.5
        out[y, z[:-1], y + 1, z[1:]] = 0.5
    return jnp.asarray(out.reshape(rows_y * zc, (rows_y + 2) * zc), jnp.bfloat16)


def prepare_kernel(per_step, cuts, rows_y, tiles, phi_ref, mix_ref, pot_ref, *out_refs):
    block = mix_ref.shape[0]
    size = block // (tiles * rows_y)
    spans = list(zip(cuts, cuts[1:]))
    singles = [0, cuts[-1] - 1] + [z for cut in cuts[1:-1] for z in (cut - 1, cut)]
    field_refs = out_refs[: len(spans) * rows_y]
    edge_ref, inner_ref = out_refs[len(spans) * rows_y : len(spans) * rows_y + 2]
    turned_pot_refs = out_refs[len(spans) * rows_y + 2 :]

    @pl.when(pl.program_id(0) == 0)
    def _():
        for y in range(rows_y):
            turned = pot_ref[:, y, :].T
            for ref, (first, last) in zip(turned_pot_refs, spans):
                ref[y * (last - first) : (y + 1) * (last - first), :] = turned[first:last]

    for step in range(per_step):
        part = phi_ref[step * block : (step + 1) * block, :]
        turned = lax.dot_general(
            part, mix_ref[...], (((0,), (0,)), ((), ())), preferred_element_type=jnp.float32
        ).astype(jnp.bfloat16)
        lanes = slice(step * size, (step + 1) * size)
        for y in range(rows_y):
            for chunk, (first, last) in enumerate(spans):
                for tile in range(tiles):
                    lo, hi = max(first, tile * LANES), min(last, (tile + 1) * LANES)
                    if lo < hi:
                        lane = (tile * rows_y + y) * size
                        field_refs[chunk * rows_y + y][lo - first : hi - first, lanes] = turned[
                            lo - tile * LANES : hi - tile * LANES, lane : lane + size
                        ]
            for k, z in enumerate(singles):
                tile, row = divmod(z, LANES)
                lane = (tile * rows_y + y) * size
                ref, at = (edge_ref, k * rows_y + y) if k < 2 else (inner_ref, (k - 2) * rows_y + y)
                ref[at : at + 1, lanes] = turned[row : row + 1, lane : lane + size]


def prepare(phi, pot, cuts):
    groups, block, rows_y, rows_z = phi.shape
    tiles = rows_z // LANES
    flat = (
        phi.reshape(groups, block, rows_y, tiles, LANES)
        .transpose(0, 1, 3, 2, 4)
        .reshape(groups * block * tiles * rows_y, LANES)
    )
    parts = tiles * rows_y
    per_step = 4
    width = per_step * block
    chunks = len(cuts) - 1
    spans = [last - first for first, last in zip(cuts, cuts[1:])]
    sizes = [span for span in spans for _ in range(rows_y)] + [2 * rows_y, 2 * rows_y * max(1, chunks - 1)]
    outs = pl.pallas_call(
        functools.partial(prepare_kernel, per_step, cuts, rows_y, tiles),
        grid=(groups // per_step,),
        in_specs=[
            pl.BlockSpec((per_step * block * parts, LANES), lambda s: (s, 0)),
            pl.BlockSpec((block * parts, block * parts), lambda s: (0, 0)),
            pl.BlockSpec((groups, rows_y, rows_z), lambda s: (0, 0, 0)),
        ],
        out_specs=[pl.BlockSpec((size, width), lambda s: (0, s)) for size in sizes]
        + [pl.BlockSpec((rows_y * span, groups), lambda s: (0, 0)) for span in spans],
        out_shape=[jax.ShapeDtypeStruct((size, groups * block), jnp.bfloat16) for size in sizes]
        + [jax.ShapeDtypeStruct((rows_y * span, groups), jnp.float32) for span in spans],
        compiler_params=pltpu.CompilerParams(vmem_limit_bytes=SCOPED),
        name="prepare",
    )(*in_hbm(flat, regroup_matrix(block, parts), pot))
    fields = [[outs[c * rows_y + y] for y in range(rows_y)] for c in range(chunks)]
    return fields, outs[chunks * rows_y], outs[chunks * rows_y + 1], outs[chunks * rows_y + 2 :]


def stacked_blocks(ref, which_ref, pair, groups):
    return jnp.concatenate(
        [
            jnp.concatenate([ref[which_ref[(2 * pair + j) * groups + row]] for j in range(2)], axis=1)
            for row in range(groups)
        ],
        axis=0,
    )


def phi_kernel(groups, rows_y, loads, which_ref, *refs):
    y_refs, refs = refs[:rows_y], refs[rows_y:]
    if loads:
        (kern_hbm, hk_hbm), (rows_ref, sum_ref, kern_ref, hk_ref, sems) = refs[:2], refs[2:]
    else:
        hk_ref, rows_ref, sum_ref = refs
    zc = y_refs[0].shape[0]
    pair = pl.program_id(0)

    def copies():
        count = kern_hbm.shape[0]
        return [
            pltpu.make_async_copy(source, target.at[:count], sems.at[k])
            for k, (source, target) in enumerate(((hk_hbm, hk_ref), (kern_hbm, kern_ref)))
        ]

    @pl.when(pair == 0)
    def _():
        if loads:
            for copy in copies():
                copy.start()
            for ref in (kern_ref, hk_ref):
                ref[ref.shape[0] - 1] = jnp.zeros(ref.shape[1:], ref.dtype)
        for y, ref in enumerate(y_refs):
            rows_ref[y * zc : (y + 1) * zc, :] = ref[...]
        if loads:
            copies()[0].wait()

    sum_ref[pair] = jnp.dot(
        rows_ref[...], stacked_blocks(hk_ref, which_ref, pair, groups), preferred_element_type=jnp.float32
    )
    if loads:

        @pl.when(pair == pl.num_programs(0) - 1)
        def _():
            copies()[1].wait()


def phi_part(fields, groups, which, kern_hk, kern=None):
    zc, width = fields[0].shape
    n = len(fields) * zc
    block = width // groups
    pairs = which.shape[0] // groups // 2
    loads = kern is not None
    hbm = pl.BlockSpec(memory_space=pltpu.HBM)
    out_shape = [pltpu.VMEM((n, width), jnp.bfloat16), pltpu.VMEM((pairs, n, 2 * block), jnp.float32)]
    if loads:
        out_shape += [pltpu.VMEM((part.shape[0] + 1, *part.shape[1:]), part.dtype) for part in (kern, kern_hk)]
    return pl.pallas_call(
        functools.partial(phi_kernel, groups, len(fields), loads),
        grid_spec=pltpu.PrefetchScalarGridSpec(
            num_scalar_prefetch=1,
            grid=(pairs,),
            in_specs=[VMEM] * len(fields) + ([hbm] * 2 if loads else [VMEM]),
            out_specs=[VMEM] * len(out_shape),
            scratch_shapes=[pltpu.SemaphoreType.DMA((2,))] if loads else [],
        ),
        out_shape=out_shape,
        compiler_params=pltpu.CompilerParams(vmem_limit_bytes=SCOPED),
        cost_estimate=pl.CostEstimate(
            flops=4 * n * width * pairs * block, transcendentals=0, bytes_accessed=2 * n * width
        ),
        name="phi_part",
    )(which, *fields, *(in_hbm(kern, kern_hk) if loads else [kern_hk]))


def fill_action(rows_y, groups, act_ref, rows, prev_ref, next_ref, low_ref, high_ref, low_at, high_at, flags, pot_ref, mix_ref):
    depth = act_ref.shape[1]
    zc = act_ref.shape[0] // rows_y
    block = depth // groups
    wide = 4
    scales = [0.5 if flag is None else 0.5 * flag.astype(jnp.float32) for flag in flags]
    for first in range(0, groups, wide):
        lanes = slice(first * block, (first + wide) * block)
        around = jnp.concatenate([prev_ref[:, lanes], rows[:, lanes], next_ref[:, lanes]], axis=0)
        beside = jnp.dot(mix_ref[...], around, preferred_element_type=jnp.float32)
        for y in range(rows_y):
            at = slice(y * zc, (y + 1) * zc)
            field = rows[at, lanes]
            pots = jnp.concatenate(
                [jnp.broadcast_to(pot_ref[at, row : row + 1], (zc, block)) for row in range(first, first + wide)],
                axis=1,
            )
            value = beside[at] - pots * field.astype(jnp.float32)
            low = scales[0] * low_ref[low_at + y : low_at + y + 1, lanes].astype(jnp.float32)
            high = scales[1] * high_ref[high_at + y : high_at + y + 1, lanes].astype(jnp.float32)
            z = lax.broadcasted_iota(jnp.int32, (8, wide * block), 0)
            head = value[:8] + jnp.where(z == 0, low, 0.0)
            tail = value[zc - 8 :] + jnp.where(z == 7, high, 0.0)
            act_ref[at, lanes] = jnp.concatenate([head, value[8 : zc - 8], tail], axis=0).astype(jnp.bfloat16)


def action_kernel(groups, rows_y, cols, low_at, high_at, masked, which_ref, *refs):
    rows_ref, sum_ref, prev_ref, next_ref, low_ref, high_ref, pot_ref, mix_ref, kern_ref, act_ref = refs[:10]
    outs = refs[10:]
    pair = pl.program_id(0)
    n = rows_ref.shape[0]
    extra = cols * groups

    @pl.when(pair == 0)
    def _():
        flags = [which_ref[extra + k] if masked[k] else None for k in range(2)]
        fill_action(
            rows_y, groups, act_ref, rows_ref, prev_ref, next_ref, low_ref, high_ref, low_at, high_at, flags, pot_ref, mix_ref
        )
        if len(outs) == 2:
            code = jnp.full((16, outs[0].shape[1]), which_ref[extra + 2].astype(jnp.float32)).astype(jnp.bfloat16)
            for ref in outs:
                ref[ref.shape[0] - 16 :, :] = code

    value = sum_ref[pair] + jnp.dot(
        act_ref[...], stacked_blocks(kern_ref, which_ref, pair, groups), preferred_element_type=jnp.float32
    )
    block = value.shape[1] // 2
    split = cols // 2 // len(outs)

    def store(ref, first):
        for j in range(2):
            at = pl.multiple_of((2 * (pair - first) + j) * n, 16)
            ref[pl.ds(at, n), :] = value[:, j * block : (j + 1) * block].astype(jnp.bfloat16)

    if len(outs) == 1:
        store(outs[0], 0)
    else:

        @pl.when(pair < split)
        def _():
            store(outs[0], 0)

        @pl.when(pair >= split)
        def _():
            store(outs[1], split)


def action_part(rows, partial, prev, below, low, low_at, high, high_at, masked, pot, groups, rows_y, cols, which, kern, halves):
    n, width = rows.shape
    zc = n // rows_y
    block = width // groups
    out_rows = [cols // halves * n + (16 if halves == 2 else 0)] * halves
    return pl.pallas_call(
        functools.partial(action_kernel, groups, rows_y, cols, low_at, high_at, masked),
        grid_spec=pltpu.PrefetchScalarGridSpec(
            num_scalar_prefetch=1,
            grid=(cols // 2,),
            in_specs=[VMEM] * 9,
            out_specs=[VMEM] * (1 + halves),
        ),
        out_shape=[pltpu.VMEM((n, width), jnp.bfloat16)]
        + [pltpu.VMEM((rows_out, block), jnp.bfloat16) for rows_out in out_rows],
        compiler_params=pltpu.CompilerParams(vmem_limit_bytes=SCOPED),
        cost_estimate=pl.CostEstimate(
            flops=2 * n * width * cols * block, transcendentals=0, bytes_accessed=2 * n * width
        ),
        name="action_part",
    )(which, rows, partial, prev, below, low, high, pot, stencil_matrix(zc, rows_y), kern)


def onward_kernel(away_ref, q0_ref, q1_ref, right_ref, right_code, left_ref, left_code, to_right, to_left):
    for mine, direction, arrived, code, out in (
        (q1_ref, RIGHT, right_ref, right_code, to_right),
        (q0_ref, LEFT, left_ref, left_code, to_left),
    ):
        kept = jnp.where(away_ref[0] == direction, mine[...].astype(jnp.float32), 0.0)
        through = code[:1, :].astype(jnp.float32) == ACROSS
        out[...] = (kept + jnp.where(through, arrived[...].astype(jnp.float32), 0.0)).astype(jnp.bfloat16)


def send_onward(away, q0, q1, right1, left1):
    rows, block = q0.shape
    steps = 4
    size = (rows - 16) // steps
    part = pl.BlockSpec((size, block), lambda s, a: (s, 0))
    code = pl.BlockSpec((16, block), lambda s, a: ((rows - 16) // 16, 0))
    return pl.pallas_call(
        onward_kernel,
        grid_spec=pltpu.PrefetchScalarGridSpec(
            num_scalar_prefetch=1,
            grid=(steps,),
            in_specs=[part, part, part, code, part, code],
            out_specs=[part, part],
        ),
        out_shape=[jax.ShapeDtypeStruct((rows - 16, block), jnp.bfloat16)] * 2,
        compiler_params=pltpu.CompilerParams(vmem_limit_bytes=SCOPED),
        cost_estimate=pl.CostEstimate(flops=0, transcendentals=0, bytes_accessed=12 * rows * block),
        name="send_onward",
    )(away, q0, q1, right1, right1, left1, left1)


def local_kernel(groups, which_ref, act_ref, rows_ref, kern_ref, hk_ref, left_ref, left_code, right_ref, right_code, out_ref):
    pair = pl.program_id(0)
    value = jnp.dot(
        act_ref[...], stacked_blocks(kern_ref, which_ref, pair, groups), preferred_element_type=jnp.float32
    ) + jnp.dot(rows_ref[...], stacked_blocks(hk_ref, which_ref, pair, groups), preferred_element_type=jnp.float32)
    n = rows_ref.shape[0]
    block = value.shape[1] // 2

    def store(arrived, code, wanted):
        mine = code[:1, :].astype(jnp.float32) == wanted
        for j in range(2):
            at = slice(j * n, (j + 1) * n)
            more = jnp.where(mine, arrived[at, :].astype(jnp.float32), 0.0)
            out_ref[at, :] = (value[:, j * block : (j + 1) * block] + more).astype(jnp.bfloat16)

    half = pl.num_programs(0) // 2

    @pl.when(pair < half)
    def _():
        store(left_ref, left_code, LEFT)

    @pl.when(pair >= half)
    def _():
        store(right_ref, right_code, RIGHT)


def local_columns(act, rows, groups, which, kern, kern_hk, left1, right1):
    cols = which.shape[0] // groups
    n, width = rows.shape
    block = width // groups
    half = cols // 4
    code = pl.BlockSpec((16, block), lambda p, w: (cols // 2 * n // 16, 0))
    return pl.pallas_call(
        functools.partial(local_kernel, groups),
        grid_spec=pltpu.PrefetchScalarGridSpec(
            num_scalar_prefetch=1,
            grid=(cols // 2,),
            in_specs=[VMEM] * 4
            + [pl.BlockSpec((2 * n, block), lambda p, w: (jnp.minimum(p, half - 1), 0)), code]
            + [pl.BlockSpec((2 * n, block), lambda p, w: (jnp.maximum(p - half, 0), 0)), code],
            out_specs=pl.BlockSpec((2 * n, block), lambda p, w: (p, 0)),
        ),
        out_shape=jax.ShapeDtypeStruct((cols * n, block), jnp.bfloat16),
        compiler_params=pltpu.CompilerParams(vmem_limit_bytes=SCOPED),
        cost_estimate=pl.CostEstimate(
            flops=4 * n * width * cols * block, transcendentals=0, bytes_accessed=2 * n * width
        ),
        name="local_columns",
    )(which, act, rows, kern, kern_hk, left1, left1, right1, right1)


def write_columns(rows_y, tiles, columns, mix_ref, out_ref):
    sizes = [value.shape[0] // rows_y for value in columns[0]]
    rows = mix_ref.shape[0]
    turned = []
    for values in columns:
        parts = []
        for tile in range(tiles):
            for y in range(rows_y):
                pieces = []
                for chunk, zc in enumerate(sizes):
                    first = sum(sizes[:chunk])
                    lo, hi = max(first, tile * LANES), min(first + zc, (tile + 1) * LANES)
                    if lo < hi:
                        pieces.append(values[chunk][y * zc + lo - first : y * zc + hi - first, :])
                part = jnp.concatenate(pieces, axis=0) if len(pieces) > 1 else pieces[0]
                parts.append((-2.0 * part).astype(jnp.bfloat16))
        turned.append(jnp.concatenate(parts, axis=1))
    wide = 2
    for first in range(0, len(turned), wide):
        both = jnp.concatenate(turned[first : first + wide], axis=0)
        out = lax.dot_general(mix_ref[...], both, (((1,), (1,)), ((), ())), preferred_element_type=jnp.float32)
        for j in range(wide):
            out_ref[(first + j) * rows : (first + j + 1) * rows, :] = out[:, j * LANES : (j + 1) * LANES].astype(
                jnp.bfloat16
            )


def final_kernel(per_step, chunks, rows_y, tiles, mix_ref, *refs):
    own, rest, out_ref = refs[:chunks], refs[chunks:-1], refs[-1]
    step = pl.program_id(0)
    half = pl.num_programs(0) // 2

    def emit(added):
        columns = []
        for col in range(per_step):
            values = []
            for chunk, mine in enumerate(own):
                n = mine.shape[0] // per_step
                at = slice(col * n, (col + 1) * n)
                value = mine[at, :].astype(jnp.float32)
                values.append(value + added[chunk][at, :].astype(jnp.float32) if added else value)
            columns.append(values)
        write_columns(rows_y, tiles, columns, mix_ref, out_ref)

    if not rest:
        emit(())
        return

    @pl.when(step < half)
    def _():
        emit(rest[:chunks])

    @pl.when(step >= half)
    def _():
        emit(rest[chunks:])


def finish(own, low, high, cols, rows_y, rows_z):
    chunks = len(own)
    block = own[0].shape[1]
    tiles = rows_z // LANES
    rows = block * tiles * rows_y
    per_step = 4
    steps = cols // per_step
    half = steps // 2

    def specs(place):
        return [pl.BlockSpec((part.shape[0] // steps, block), lambda s: (place(s), 0)) for part in own]

    in_specs = [pl.BlockSpec((rows, rows), lambda s: (0, 0))] + specs(lambda s: s)
    arrays = list(own)
    if low is not None:
        in_specs += specs(lambda s: jnp.minimum(s, half - 1)) + specs(lambda s: jnp.maximum(s - half, 0))
        arrays += [*low, *high]
    flat = pl.pallas_call(
        functools.partial(final_kernel, per_step, chunks, rows_y, tiles),
        grid=(steps,),
        in_specs=in_specs,
        out_specs=pl.BlockSpec((per_step * rows, LANES), lambda s: (s, 0)),
        out_shape=jax.ShapeDtypeStruct((cols * rows, LANES), jnp.bfloat16),
        compiler_params=pltpu.CompilerParams(vmem_limit_bytes=SCOPED),
        name="finish",
    )(*in_hbm(regroup_matrix(block, tiles * rows_y), *arrays))
    return unflatten(flat, cols, block, rows_y, tiles)


def unflatten(flat, cols, block, rows_y, tiles):
    return (
        flat.reshape(cols, block, tiles, rows_y, LANES)
        .transpose(0, 1, 3, 2, 4)
        .reshape(cols, block, rows_y, tiles * LANES)
    )


def block_of_column(slot_of, slots):
    hit = slot_of[None, :, :] == slots[:, None, None]
    zero = slot_of.size
    place = jnp.arange(zero, dtype=jnp.int32).reshape(slot_of.shape) - zero
    return zero + jnp.sum(jnp.where(hit, place, 0), axis=2)


def shifts(axis, by):
    count = lax.axis_size(axis)
    return [(i, i + by) for i in range(count) if 0 <= i + by < count]


def outer_rows(edges, rows_y):
    if lax.axis_size("gz") == 2:
        return lax.ppermute(edges, "gz", [(0, 1), (1, 0)])
    after_last = lax.ppermute(edges[:rows_y], "gz", shifts("gz", -1))
    before_first = lax.ppermute(edges[rows_y:], "gz", shifts("gz", 1))
    return jnp.concatenate([after_last, before_first], axis=0)


def per_device(phi, pot, kern, kern_hk, slot_of, req_cols):
    groups, block, rows_y, rows_z = phi.shape
    listed = req_cols.shape[0]
    ring = lax.axis_size("gx")
    cuts = CUTS if CUTS[-1] == rows_z else (0, rows_z)
    chunks = len(cuts) - 1

    fields, edges, inner, pots = prepare(phi, pot, cuts)
    halo = []

    def send_halo(c, *before):
        up, down = after(fields[c][-1], *before), after(fields[c][0], *before)
        halo.append((lax.ppermute(up, "gy", shifts("gy", 1)), lax.ppermute(down, "gy", shifts("gy", -1))))

    send_halo(0)
    outer = outer_rows(edges, rows_y)
    req_cols, slot_of, _ = lax.optimization_barrier((req_cols, slot_of, edges))
    kern = kern.reshape(-1, block, block)
    kern_hk = kern_hk.reshape(-1, block, block)
    place = lax.axis_index("gz")
    marks = [place > 0, place < lax.axis_size("gz") - 1]

    def sides(c):
        low = (outer, rows_y) if c == 0 else (inner, (2 * c - 2) * rows_y)
        high = (outer, 0) if c == chunks - 1 else (inner, (2 * c + 1) * rows_y)
        return *low, *high, (c == 0, c == chunks - 1)

    blocks = []

    def phi_columns(c, names):
        if blocks:
            return phi_part(fields[c], groups, names, blocks[1])
        mine, partial, *loaded = phi_part(fields[c], groups, names, kern_hk, kern)
        blocks.extend(loaded)
        return mine, partial

    def all_columns(c, mine, partial, table, cols, halves):
        return action_part(
            mine, partial, *halo[c], *sides(c), pots[c], groups, rows_y, cols, table, blocks[0], halves
        )

    if ring != 4:
        which = block_of_column(slot_of, jnp.arange(listed, dtype=jnp.int32)).reshape(-1)
        table = jnp.concatenate([which, jnp.stack(marks).astype(jnp.int32)])
        hit = req_cols[None, :] == jnp.arange(groups * ring, dtype=jnp.int32)[:, None]
        named = jnp.any(hit, axis=1)
        source = jnp.sum(jnp.where(hit, jnp.arange(listed, dtype=jnp.int32), 0), axis=1)
        parts = []
        for c in range(chunks):
            if c:
                send_halo(c, table)
            _, sums = all_columns(c, *phi_columns(c, which), table, listed, 1)
            spread = jnp.where(named[:, None, None], sums.reshape(listed, -1, block)[source], 0)
            total = lax.psum_scatter(spread, "gx", scatter_dimension=0, tiled=True)
            parts.append(total.reshape(-1, block))
        return finish(parts, None, None, groups, rows_y, rows_z)

    me = lax.axis_index("gx")
    owners = req_cols // groups
    other = jnp.where(owners[0] == me, owners[listed - 1], owners[0])
    away = (other - me) % ring
    ahead = [(i, (i + 1) % ring) for i in range(ring)]
    behind = [(i, (i - 1) % ring) for i in range(ring)]

    half = groups // 2
    column = jnp.arange(groups, dtype=jnp.int32)
    swapped = jnp.where(away == ACROSS, column, (column + half) % groups)
    wanted = jnp.concatenate([other * groups + swapped, me * groups + column])
    slots = jnp.sum(
        jnp.where(wanted[:, None] == req_cols[None, :], jnp.arange(listed, dtype=jnp.int32), 0), axis=1
    )
    which = block_of_column(slot_of, slots).reshape(-1)
    far, near = which[: groups * groups], which[groups * groups :]
    table = jnp.concatenate([far, jnp.stack([*marks, away]).astype(jnp.int32)])
    away = away.reshape(1)
    for c in range(1, chunks):
        send_halo(c, table)

    rows, acts, sent, own, right1, left1, right2, left2 = [], [], [], [], [], [], [], []

    def send_first(c, *before):
        mine, partial = phi_columns(c, after(far, *before))
        act, q0, q1 = all_columns(c, mine, partial, after(table, *before), groups, 2)
        rows.append(mine)
        acts.append(act)
        sent.append((q0, q1))
        right1.append(lax.ppermute(q0, "gx", ahead))
        left1.append(lax.ppermute(q1, "gx", behind))

    def send_second(c, *before):
        arrived = lax.optimization_barrier((right1[c], left1[c], *before))
        right1[c], left1[c] = arrived[:2]
        to_right, to_left = send_onward(away, *sent[c], right1[c], left1[c])
        right2.append(lax.ppermute(to_right, "gx", ahead))
        left2.append(lax.ppermute(to_left, "gx", behind))
        own.append(
            local_columns(acts[c], rows[c], groups, after(near, to_right, *right2[:c], *left2[:c]), *blocks, left1[c], right1[c])
        )

    send_first(0)
    for c in range(1, chunks):
        send_first(c, *sent[c - 1])
        send_second(c - 1, *sent[c])
    send_second(chunks - 1, own[-1])
    return finish(own, right2, left2, groups, rows_y, rows_z)


def solution(mesh):
    placed = (
        P("gx", None, "gy", "gz"),
        P("gx", "gy", "gz"),
        P("gx", None, None, None),
        P("gx", None, None, None),
        P("gx", None),
        P("gx"),
    )
    return jax.shard_map(
        per_device, mesh=mesh, in_specs=placed, out_specs=P("gx", None, "gy", "gz"), check_vma=False
    )
```

```python
import functools

import jax
import jax.numpy as jnp
import numpy as np
from jax import lax
from jax.experimental import pallas as pl
from jax.experimental.pallas import tpu as pltpu
from jax.sharding import PartitionSpec as P

CUTS = (0, 96, 176, 256)
RIGHT, ACROSS, LEFT = 1, 2, 3
LANES = 128
SCOPED = 8 << 20
VMEM = pl.BlockSpec(memory_space=pltpu.VMEM)


def hinted(flops):
    return flops // 4


def in_hbm(*arrays):
    return [pltpu.with_memory_space_constraint(array, pltpu.HBM) for array in arrays]


def after(value, *before):
    return lax.optimization_barrier((value, *before))[0]


def regroup_matrix(block, parts):
    rows = np.arange(block * parts)
    out = np.zeros((block * parts, block * parts), np.float32)
    out[rows, (rows % parts) * block + rows // parts] = 1.0
    return jnp.asarray(out, jnp.bfloat16)


def stencil_matrix(zc, rows_y):
    out = np.zeros((rows_y, zc, rows_y + 2, zc), np.float32)
    z = np.arange(zc)
    for y in range(rows_y):
        out[y, z, y, z] = 0.5
        out[y, z, y + 2, z] = 0.5
        out[y, z, y + 1, z] = -2.0
        out[y, z[1:], y + 1, z[:-1]] = 0.5
        out[y, z[:-1], y + 1, z[1:]] = 0.5
    return jnp.asarray(out.reshape(rows_y * zc, (rows_y + 2) * zc), jnp.bfloat16)


def prepare_kernel(per_step, cuts, rows_y, tiles, phi_ref, mix_ref, pot_ref, *out_refs):
    block = mix_ref.shape[0]
    size = block // (tiles * rows_y)
    spans = list(zip(cuts, cuts[1:]))
    singles = [0, cuts[-1] - 1] + [z for cut in cuts[1:-1] for z in (cut - 1, cut)]
    field_refs = out_refs[: len(spans) * rows_y]
    edge_ref, inner_ref = out_refs[len(spans) * rows_y : len(spans) * rows_y + 2]
    turned_pot_refs = out_refs[len(spans) * rows_y + 2 :]

    @pl.when(pl.program_id(0) == 0)
    def _():
        for y in range(rows_y):
            turned = pot_ref[:, y, :].T
            for ref, (first, last) in zip(turned_pot_refs, spans):
                ref[y * (last - first) : (y + 1) * (last - first), :] = turned[first:last]

    for step in range(per_step):
        part = phi_ref[step * block : (step + 1) * block, :]
        turned = lax.dot_general(
            part, mix_ref[...], (((0,), (0,)), ((), ())), preferred_element_type=jnp.float32
        ).astype(jnp.bfloat16)
        lanes = slice(step * size, (step + 1) * size)
        for y in range(rows_y):
            for chunk, (first, last) in enumerate(spans):
                for tile in range(tiles):
                    lo, hi = max(first, tile * LANES), min(last, (tile + 1) * LANES)
                    if lo < hi:
                        lane = (tile * rows_y + y) * size
                        field_refs[chunk * rows_y + y][lo - first : hi - first, lanes] = turned[
                            lo - tile * LANES : hi - tile * LANES, lane : lane + size
                        ]
            for k, z in enumerate(singles):
                tile, row = divmod(z, LANES)
                lane = (tile * rows_y + y) * size
                ref, at = (edge_ref, k * rows_y + y) if k < 2 else (inner_ref, (k - 2) * rows_y + y)
                ref[at : at + 1, lanes] = turned[row : row + 1, lane : lane + size]


def prepare(phi, pot, cuts):
    groups, block, rows_y, rows_z = phi.shape
    tiles = rows_z // LANES
    flat = (
        phi.reshape(groups, block, rows_y, tiles, LANES)
        .transpose(0, 1, 3, 2, 4)
        .reshape(groups * block * tiles * rows_y, LANES)
    )
    parts = tiles * rows_y
    per_step = 4
    width = per_step * block
    chunks = len(cuts) - 1
    spans = [last - first for first, last in zip(cuts, cuts[1:])]
    sizes = [span for span in spans for _ in range(rows_y)] + [2 * rows_y, 2 * rows_y * max(1, chunks - 1)]
    outs = pl.pallas_call(
        functools.partial(prepare_kernel, per_step, cuts, rows_y, tiles),
        grid=(groups // per_step,),
        in_specs=[
            pl.BlockSpec((per_step * block * parts, LANES), lambda s: (s, 0)),
            pl.BlockSpec((block * parts, block * parts), lambda s: (0, 0)),
            pl.BlockSpec((groups, rows_y, rows_z), lambda s: (0, 0, 0)),
        ],
        out_specs=[pl.BlockSpec((size, width), lambda s: (0, s)) for size in sizes]
        + [pl.BlockSpec((rows_y * span, groups), lambda s: (0, 0)) for span in spans],
        out_shape=[jax.ShapeDtypeStruct((size, groups * block), jnp.bfloat16) for size in sizes]
        + [jax.ShapeDtypeStruct((rows_y * span, groups), jnp.float32) for span in spans],
        compiler_params=pltpu.CompilerParams(vmem_limit_bytes=SCOPED),
        name="prepare",
    )(*in_hbm(flat, regroup_matrix(block, parts), pot))
    fields = [[outs[c * rows_y + y] for y in range(rows_y)] for c in range(chunks)]
    return fields, outs[chunks * rows_y], outs[chunks * rows_y + 1], outs[chunks * rows_y + 2 :]


def stacked_blocks(ref, which_ref, pair, groups):
    return jnp.concatenate(
        [
            jnp.concatenate([ref[which_ref[(2 * pair + j) * groups + row]] for j in range(2)], axis=1)
            for row in range(groups)
        ],
        axis=0,
    )


def phi_kernel(groups, rows_y, loads, which_ref, *refs):
    y_refs, refs = refs[:rows_y], refs[rows_y:]
    if loads:
        (kern_hbm, hk_hbm), (rows_ref, sum_ref, kern_ref, hk_ref, sems) = refs[:2], refs[2:]
    else:
        hk_ref, rows_ref, sum_ref = refs
    zc = y_refs[0].shape[0]
    pair = pl.program_id(0)

    def copies():
        count = kern_hbm.shape[0]
        return [
            pltpu.make_async_copy(source, target.at[:count], sems.at[k])
            for k, (source, target) in enumerate(((hk_hbm, hk_ref), (kern_hbm, kern_ref)))
        ]

    @pl.when(pair == 0)
    def _():
        if loads:
            for copy in copies():
                copy.start()
            for ref in (kern_ref, hk_ref):
                ref[ref.shape[0] - 1] = jnp.zeros(ref.shape[1:], ref.dtype)
        for y, ref in enumerate(y_refs):
            rows_ref[y * zc : (y + 1) * zc, :] = ref[...]
        if loads:
            copies()[0].wait()

    sum_ref[pair] = jnp.dot(
        rows_ref[...], stacked_blocks(hk_ref, which_ref, pair, groups), preferred_element_type=jnp.float32
    )
    if loads:

        @pl.when(pair == pl.num_programs(0) - 1)
        def _():
            copies()[1].wait()


def phi_part(fields, groups, which, kern_hk, kern=None):
    zc, width = fields[0].shape
    n = len(fields) * zc
    block = width // groups
    pairs = which.shape[0] // groups // 2
    loads = kern is not None
    hbm = pl.BlockSpec(memory_space=pltpu.HBM)
    out_shape = [pltpu.VMEM((n, width), jnp.bfloat16), pltpu.VMEM((pairs, n, 2 * block), jnp.float32)]
    if loads:
        out_shape += [pltpu.VMEM((part.shape[0] + 1, *part.shape[1:]), part.dtype) for part in (kern, kern_hk)]
    return pl.pallas_call(
        functools.partial(phi_kernel, groups, len(fields), loads),
        grid_spec=pltpu.PrefetchScalarGridSpec(
            num_scalar_prefetch=1,
            grid=(pairs,),
            in_specs=[VMEM] * len(fields) + ([hbm] * 2 if loads else [VMEM]),
            out_specs=[VMEM] * len(out_shape),
            scratch_shapes=[pltpu.SemaphoreType.DMA((2,))] if loads else [],
        ),
        out_shape=out_shape,
        compiler_params=pltpu.CompilerParams(vmem_limit_bytes=SCOPED),
        cost_estimate=pl.CostEstimate(
            flops=hinted(4 * n * width * pairs * block), transcendentals=0, bytes_accessed=2 * n * width
        ),
        name="phi_part",
    )(which, *fields, *(in_hbm(kern, kern_hk) if loads else [kern_hk]))


def fill_action(rows_y, groups, act_ref, rows, prev_ref, next_ref, low_ref, high_ref, low_at, high_at, flags, pot_ref, mix_ref):
    depth = act_ref.shape[1]
    zc = act_ref.shape[0] // rows_y
    block = depth // groups
    wide = 4
    scales = [0.5 if flag is None else 0.5 * flag.astype(jnp.float32) for flag in flags]
    for first in range(0, groups, wide):
        lanes = slice(first * block, (first + wide) * block)
        around = jnp.concatenate([prev_ref[:, lanes], rows[:, lanes], next_ref[:, lanes]], axis=0)
        beside = jnp.dot(mix_ref[...], around, preferred_element_type=jnp.float32)
        for y in range(rows_y):
            at = slice(y * zc, (y + 1) * zc)
            field = rows[at, lanes]
            pots = jnp.concatenate(
                [jnp.broadcast_to(pot_ref[at, row : row + 1], (zc, block)) for row in range(first, first + wide)],
                axis=1,
            )
            value = beside[at] - pots * field.astype(jnp.float32)
            low = scales[0] * low_ref[low_at + y : low_at + y + 1, lanes].astype(jnp.float32)
            high = scales[1] * high_ref[high_at + y : high_at + y + 1, lanes].astype(jnp.float32)
            z = lax.broadcasted_iota(jnp.int32, (8, wide * block), 0)
            head = value[:8] + jnp.where(z == 0, low, 0.0)
            tail = value[zc - 8 :] + jnp.where(z == 7, high, 0.0)
            act_ref[at, lanes] = jnp.concatenate([head, value[8 : zc - 8], tail], axis=0).astype(jnp.bfloat16)


def action_kernel(groups, rows_y, cols, low_at, high_at, masked, which_ref, *refs):
    rows_ref, sum_ref, prev_ref, next_ref, low_ref, high_ref, pot_ref, mix_ref, kern_ref, act_ref = refs[:10]
    outs = refs[10:]
    pair = pl.program_id(0)
    n = rows_ref.shape[0]
    extra = cols * groups

    @pl.when(pair == 0)
    def _():
        flags = [which_ref[extra + k] if masked[k] else None for k in range(2)]
        fill_action(
            rows_y, groups, act_ref, rows_ref, prev_ref, next_ref, low_ref, high_ref, low_at, high_at, flags, pot_ref, mix_ref
        )
        if len(outs) == 2:
            code = jnp.full((16, outs[0].shape[1]), which_ref[extra + 2].astype(jnp.float32)).astype(jnp.bfloat16)
            for ref in outs:
                ref[ref.shape[0] - 16 :, :] = code

    value = sum_ref[pair] + jnp.dot(
        act_ref[...], stacked_blocks(kern_ref, which_ref, pair, groups), preferred_element_type=jnp.float32
    )
    block = value.shape[1] // 2
    split = cols // 2 // len(outs)

    def store(ref, first):
        for j in range(2):
            at = pl.multiple_of((2 * (pair - first) + j) * n, 16)
            ref[pl.ds(at, n), :] = value[:, j * block : (j + 1) * block].astype(jnp.bfloat16)

    if len(outs) == 1:
        store(outs[0], 0)
    else:

        @pl.when(pair < split)
        def _():
            store(outs[0], 0)

        @pl.when(pair >= split)
        def _():
            store(outs[1], split)


def action_part(rows, partial, prev, below, low, low_at, high, high_at, masked, pot, groups, rows_y, cols, which, kern, halves):
    n, width = rows.shape
    zc = n // rows_y
    block = width // groups
    out_rows = [cols // halves * n + (16 if halves == 2 else 0)] * halves
    return pl.pallas_call(
        functools.partial(action_kernel, groups, rows_y, cols, low_at, high_at, masked),
        grid_spec=pltpu.PrefetchScalarGridSpec(
            num_scalar_prefetch=1,
            grid=(cols // 2,),
            in_specs=[VMEM] * 9,
            out_specs=[VMEM] * (1 + halves),
        ),
        out_shape=[pltpu.VMEM((n, width), jnp.bfloat16)]
        + [pltpu.VMEM((rows_out, block), jnp.bfloat16) for rows_out in out_rows],
        compiler_params=pltpu.CompilerParams(vmem_limit_bytes=SCOPED),
        cost_estimate=pl.CostEstimate(
            flops=hinted(2 * n * width * cols * block), transcendentals=0, bytes_accessed=2 * n * width
        ),
        name="action_part",
    )(which, rows, partial, prev, below, low, high, pot, stencil_matrix(zc, rows_y), kern)


def onward_kernel(away_ref, q0_ref, q1_ref, right_ref, right_code, left_ref, left_code, to_right, to_left):
    for mine, direction, arrived, code, out in (
        (q1_ref, RIGHT, right_ref, right_code, to_right),
        (q0_ref, LEFT, left_ref, left_code, to_left),
    ):
        kept = jnp.where(away_ref[0] == direction, mine[...].astype(jnp.float32), 0.0)
        through = code[:1, :].astype(jnp.float32) == ACROSS
        out[...] = (kept + jnp.where(through, arrived[...].astype(jnp.float32), 0.0)).astype(jnp.bfloat16)


def send_onward(away, q0, q1, right1, left1):
    rows, block = q0.shape
    steps = 4
    size = (rows - 16) // steps
    part = pl.BlockSpec((size, block), lambda s, a: (s, 0))
    code = pl.BlockSpec((16, block), lambda s, a: ((rows - 16) // 16, 0))
    return pl.pallas_call(
        onward_kernel,
        grid_spec=pltpu.PrefetchScalarGridSpec(
            num_scalar_prefetch=1,
            grid=(steps,),
            in_specs=[part, part, part, code, part, code],
            out_specs=[part, part],
        ),
        out_shape=[jax.ShapeDtypeStruct((rows - 16, block), jnp.bfloat16)] * 2,
        compiler_params=pltpu.CompilerParams(vmem_limit_bytes=SCOPED),
        cost_estimate=pl.CostEstimate(flops=0, transcendentals=0, bytes_accessed=12 * rows * block),
        name="send_onward",
    )(away, q0, q1, right1, right1, left1, left1)


def local_kernel(groups, which_ref, act_ref, rows_ref, kern_ref, hk_ref, left_ref, left_code, right_ref, right_code, out_ref):
    pair = pl.program_id(0)
    value = jnp.dot(
        act_ref[...], stacked_blocks(kern_ref, which_ref, pair, groups), preferred_element_type=jnp.float32
    ) + jnp.dot(rows_ref[...], stacked_blocks(hk_ref, which_ref, pair, groups), preferred_element_type=jnp.float32)
    n = rows_ref.shape[0]
    block = value.shape[1] // 2

    def store(arrived, code, wanted):
        mine = code[:1, :].astype(jnp.float32) == wanted
        for j in range(2):
            at = slice(j * n, (j + 1) * n)
            more = jnp.where(mine, arrived[at, :].astype(jnp.float32), 0.0)
            out_ref[at, :] = (value[:, j * block : (j + 1) * block] + more).astype(jnp.bfloat16)

    half = pl.num_programs(0) // 2

    @pl.when(pair < half)
    def _():
        store(left_ref, left_code, LEFT)

    @pl.when(pair >= half)
    def _():
        store(right_ref, right_code, RIGHT)


def local_columns(act, rows, groups, which, kern, kern_hk, left1, right1):
    cols = which.shape[0] // groups
    n, width = rows.shape
    block = width // groups
    half = cols // 4
    code = pl.BlockSpec((16, block), lambda p, w: (cols // 2 * n // 16, 0))
    return pl.pallas_call(
        functools.partial(local_kernel, groups),
        grid_spec=pltpu.PrefetchScalarGridSpec(
            num_scalar_prefetch=1,
            grid=(cols // 2,),
            in_specs=[VMEM] * 4
            + [pl.BlockSpec((2 * n, block), lambda p, w: (jnp.minimum(p, half - 1), 0)), code]
            + [pl.BlockSpec((2 * n, block), lambda p, w: (jnp.maximum(p - half, 0), 0)), code],
            out_specs=pl.BlockSpec((2 * n, block), lambda p, w: (p, 0)),
        ),
        out_shape=jax.ShapeDtypeStruct((cols * n, block), jnp.bfloat16),
        compiler_params=pltpu.CompilerParams(vmem_limit_bytes=SCOPED),
        cost_estimate=pl.CostEstimate(
            flops=hinted(4 * n * width * cols * block), transcendentals=0, bytes_accessed=2 * n * width
        ),
        name="local_columns",
    )(which, act, rows, kern, kern_hk, left1, left1, right1, right1)


def write_columns(rows_y, tiles, columns, mix_ref, out_ref):
    sizes = [value.shape[0] // rows_y for value in columns[0]]
    rows = mix_ref.shape[0]
    turned = []
    for values in columns:
        parts = []
        for tile in range(tiles):
            for y in range(rows_y):
                pieces = []
                for chunk, zc in enumerate(sizes):
                    first = sum(sizes[:chunk])
                    lo, hi = max(first, tile * LANES), min(first + zc, (tile + 1) * LANES)
                    if lo < hi:
                        pieces.append(values[chunk][y * zc + lo - first : y * zc + hi - first, :])
                part = jnp.concatenate(pieces, axis=0) if len(pieces) > 1 else pieces[0]
                parts.append((-2.0 * part).astype(jnp.bfloat16))
        turned.append(jnp.concatenate(parts, axis=1))
    wide = 2
    for first in range(0, len(turned), wide):
        both = jnp.concatenate(turned[first : first + wide], axis=0)
        out = lax.dot_general(mix_ref[...], both, (((1,), (1,)), ((), ())), preferred_element_type=jnp.float32)
        for j in range(wide):
            out_ref[(first + j) * rows : (first + j + 1) * rows, :] = out[:, j * LANES : (j + 1) * LANES].astype(
                jnp.bfloat16
            )


def final_kernel(per_step, counts, rows_y, tiles, mix_ref, *refs):
    out_ref = refs[-1]
    columns = []
    for col in range(per_step):
        values, first = [], 0
        for count in counts:
            n = refs[first].shape[0] // per_step
            at = slice(col * n, (col + 1) * n)
            values.append(sum(ref[at, :].astype(jnp.float32) for ref in refs[first : first + count]))
            first += count
        columns.append(values)
    write_columns(rows_y, tiles, columns, mix_ref, out_ref)


def finish(parts, firsts, cols, all_cols, rows_y, rows_z, before=None):
    arrays = [array for part in parts for array in part]
    block = arrays[0].shape[1]
    tiles = rows_z // LANES
    rows = block * tiles * rows_y
    per_step = 4
    start = firsts[0] // per_step
    in_specs = [pl.BlockSpec((rows, rows), lambda s: (0, 0))]
    for part in parts:
        n = part[0].shape[0] // all_cols
        for first, _ in zip(firsts, part):
            in_specs.append(
                pl.BlockSpec((per_step * n, block), functools.partial(lambda at, s: (s + at, 0), first // per_step))
            )
    arrays = in_hbm(regroup_matrix(block, tiles * rows_y), *arrays)
    counts = [len(part) for part in parts]
    kernel = functools.partial(final_kernel, per_step, counts, rows_y, tiles)
    aliases = {}
    if before is not None:
        aliases = {len(arrays): 0}
        arrays.append(before)
        in_specs.append(pl.BlockSpec(memory_space=pl.ANY))
        kernel = lambda *refs: final_kernel(per_step, counts, rows_y, tiles, *refs[:-2], refs[-1])
    return pl.pallas_call(
        kernel,
        grid=(cols // per_step,),
        in_specs=in_specs,
        out_specs=pl.BlockSpec((per_step * rows, LANES), lambda s: (s + start, 0)),
        out_shape=jax.ShapeDtypeStruct((all_cols * rows, LANES), jnp.bfloat16),
        input_output_aliases=aliases,
        compiler_params=pltpu.CompilerParams(vmem_limit_bytes=SCOPED),
        name="finish",
    )(*arrays)


def unflatten(flat, cols, block, rows_y, tiles):
    return (
        flat.reshape(cols, block, tiles, rows_y, LANES)
        .transpose(0, 1, 3, 2, 4)
        .reshape(cols, block, rows_y, tiles * LANES)
    )


def block_of_column(slot_of, slots):
    hit = slot_of[None, :, :] == slots[:, None, None]
    zero = slot_of.size
    place = jnp.arange(zero, dtype=jnp.int32).reshape(slot_of.shape) - zero
    return zero + jnp.sum(jnp.where(hit, place, 0), axis=2)


def shifts(axis, by):
    count = lax.axis_size(axis)
    return [(i, i + by) for i in range(count) if 0 <= i + by < count]


def outer_rows(edges, rows_y):
    if lax.axis_size("gz") == 2:
        return lax.ppermute(edges, "gz", [(0, 1), (1, 0)])
    after_last = lax.ppermute(edges[:rows_y], "gz", shifts("gz", -1))
    before_first = lax.ppermute(edges[rows_y:], "gz", shifts("gz", 1))
    return jnp.concatenate([after_last, before_first], axis=0)


def per_device(phi, pot, kern, kern_hk, slot_of, req_cols):
    groups, block, rows_y, rows_z = phi.shape
    listed = req_cols.shape[0]
    ring = lax.axis_size("gx")
    cuts = CUTS if CUTS[-1] == rows_z else (0, rows_z)
    chunks = len(cuts) - 1

    fields, edges, inner, pots = prepare(phi, pot, cuts)
    halo = []

    def send_halo(c, *before):
        up, down = after(fields[c][-1], *before), after(fields[c][0], *before)
        halo.append((lax.ppermute(up, "gy", shifts("gy", 1)), lax.ppermute(down, "gy", shifts("gy", -1))))

    send_halo(0)
    outer = outer_rows(edges, rows_y)
    req_cols, slot_of, _ = lax.optimization_barrier((req_cols, slot_of, edges))
    kern = kern.reshape(-1, block, block)
    kern_hk = kern_hk.reshape(-1, block, block)
    place = lax.axis_index("gz")
    marks = [place > 0, place < lax.axis_size("gz") - 1]

    def sides(c):
        low = (outer, rows_y) if c == 0 else (inner, (2 * c - 2) * rows_y)
        high = (outer, 0) if c == chunks - 1 else (inner, (2 * c + 1) * rows_y)
        return *low, *high, (c == 0, c == chunks - 1)

    blocks = []

    def phi_columns(c, names):
        if blocks:
            return phi_part(fields[c], groups, names, blocks[1])
        mine, partial, *loaded = phi_part(fields[c], groups, names, kern_hk, kern)
        blocks.extend(loaded)
        return mine, partial

    def all_columns(c, mine, partial, table, cols, halves):
        return action_part(
            mine, partial, *halo[c], *sides(c), pots[c], groups, rows_y, cols, table, blocks[0], halves
        )

    if ring != 4:
        which = block_of_column(slot_of, jnp.arange(listed, dtype=jnp.int32)).reshape(-1)
        table = jnp.concatenate([which, jnp.stack(marks).astype(jnp.int32)])
        hit = req_cols[None, :] == jnp.arange(groups * ring, dtype=jnp.int32)[:, None]
        named = jnp.any(hit, axis=1)
        source = jnp.sum(jnp.where(hit, jnp.arange(listed, dtype=jnp.int32), 0), axis=1)
        parts = []
        for c in range(chunks):
            if c:
                send_halo(c, table)
            _, sums = all_columns(c, *phi_columns(c, which), table, listed, 1)
            spread = jnp.where(named[:, None, None], sums.reshape(listed, -1, block)[source], 0)
            total = lax.psum_scatter(spread, "gx", scatter_dimension=0, tiled=True)
            parts.append([total.reshape(-1, block)])
        flat = finish(parts, (0,), groups, groups, rows_y, rows_z)
        return unflatten(flat, groups, block, rows_y, rows_z // LANES)

    me = lax.axis_index("gx")
    owners = req_cols // groups
    other = jnp.where(owners[0] == me, owners[listed - 1], owners[0])
    away = (other - me) % ring
    ahead = [(i, (i + 1) % ring) for i in range(ring)]
    behind = [(i, (i - 1) % ring) for i in range(ring)]

    half = groups // 2
    column = jnp.arange(groups, dtype=jnp.int32)
    swapped = jnp.where(away == ACROSS, column, (column + half) % groups)
    wanted = jnp.concatenate([other * groups + swapped, me * groups + column])
    slots = jnp.sum(
        jnp.where(wanted[:, None] == req_cols[None, :], jnp.arange(listed, dtype=jnp.int32), 0), axis=1
    )
    which = block_of_column(slot_of, slots).reshape(-1)
    far, near = which[: groups * groups], which[groups * groups :]
    table = jnp.concatenate([far, jnp.stack([*marks, away]).astype(jnp.int32)])
    away = away.reshape(1)
    send_halo(1, table)

    rows, acts, sent, own, right1, left1, right2, left2 = [], [], [], [], [], [], [], []

    def send_first(c, *before):
        mine, partial = phi_columns(c, after(far, *before))
        act, q0, q1 = all_columns(c, mine, partial, after(table, *before), groups, 2)
        rows.append(mine)
        acts.append(act)
        sent.append((q0, q1))
        right1.append(lax.ppermute(q0, "gx", ahead))
        left1.append(lax.ppermute(q1, "gx", behind))

    def send_second(c, *before):
        arrived = lax.optimization_barrier((right1[c], left1[c], *before))
        right1[c], left1[c] = arrived[:2]
        to_right, to_left = send_onward(away, *sent[c], right1[c], left1[c])
        right2.append(lax.ppermute(to_right, "gx", ahead))
        left2.append(lax.ppermute(to_left, "gx", behind))
        own.append(
            local_columns(acts[c], rows[c], groups, after(near, to_right, *right2[:c], *left2[:c]), *blocks, left1[c], right1[c])
        )

    send_first(0)
    for c in range(1, chunks):
        if c + 1 < chunks:
            send_halo(c + 1, sent[c - 1][1])
        send_first(c, *sent[c - 1])
        send_second(c - 1, *sent[c])
    send_second(chunks - 1, own[-1])
    flat = finish(list(zip(own, right2)), (0, 0), half, groups, rows_y, rows_z)
    left2 = lax.optimization_barrier((*left2, flat))
    flat = finish(list(zip(own, left2)), (half, 0), half, groups, rows_y, rows_z, left2[-1])
    return unflatten(flat, groups, block, rows_y, rows_z // LANES)


def solution(mesh):
    placed = (
        P("gx", None, "gy", "gz"),
        P("gx", "gy", "gz"),
        P("gx", None, None, None),
        P("gx", None, None, None),
        P("gx", None),
        P("gx"),
    )
    return jax.shard_map(
        per_device, mesh=mesh, in_specs=placed, out_specs=P("gx", None, "gy", "gz"), check_vma=False
    )
```

```python
import functools

import jax
import jax.numpy as jnp
import numpy as np
from jax import lax
from jax.experimental import pallas as pl
from jax.experimental.pallas import tpu as pltpu
from jax.sharding import PartitionSpec as P

CUTS = (0, 96, 176, 256)
RIGHT, ACROSS, LEFT = 1, 2, 3
LANES = 128
SCOPED = 8 << 20
VMEM = pl.BlockSpec(memory_space=pltpu.VMEM)


def hinted(flops):
    return flops // 4


def in_hbm(*arrays):
    return [pltpu.with_memory_space_constraint(array, pltpu.HBM) for array in arrays]


def after(value, *before):
    return lax.optimization_barrier((value, *before))[0]


def regroup_matrix(block, parts):
    rows = np.arange(block * parts)
    out = np.zeros((block * parts, block * parts), np.float32)
    out[rows, (rows % parts) * block + rows // parts] = 1.0
    return jnp.asarray(out, jnp.bfloat16)


def stencil_matrix(zc, rows_y):
    out = np.zeros((rows_y, zc, rows_y + 2, zc), np.float32)
    z = np.arange(zc)
    for y in range(rows_y):
        out[y, z, y, z] = 0.5
        out[y, z, y + 2, z] = 0.5
        out[y, z, y + 1, z] = -2.0
        out[y, z[1:], y + 1, z[:-1]] = 0.5
        out[y, z[:-1], y + 1, z[1:]] = 0.5
    return jnp.asarray(out.reshape(rows_y * zc, (rows_y + 2) * zc), jnp.bfloat16)


def prepare_kernel(per_step, cuts, rows_y, tiles, phi_ref, mix_ref, pot_ref, *out_refs):
    block = mix_ref.shape[0]
    size = block // (tiles * rows_y)
    spans = list(zip(cuts, cuts[1:]))
    singles = [0, cuts[-1] - 1] + [z for cut in cuts[1:-1] for z in (cut - 1, cut)]
    field_refs = out_refs[: len(spans) * rows_y]
    edge_ref, inner_ref = out_refs[len(spans) * rows_y : len(spans) * rows_y + 2]
    turned_pot_refs = out_refs[len(spans) * rows_y + 2 :]

    @pl.when(pl.program_id(0) == 0)
    def _():
        for y in range(rows_y):
            turned = pot_ref[:, y, :].T
            for ref, (first, last) in zip(turned_pot_refs, spans):
                ref[y * (last - first) : (y + 1) * (last - first), :] = turned[first:last]

    for step in range(per_step):
        part = phi_ref[step * block : (step + 1) * block, :]
        turned = lax.dot_general(
            part, mix_ref[...], (((0,), (0,)), ((), ())), preferred_element_type=jnp.float32
        ).astype(jnp.bfloat16)
        lanes = slice(step * size, (step + 1) * size)
        for y in range(rows_y):
            for chunk, (first, last) in enumerate(spans):
                for tile in range(tiles):
                    lo, hi = max(first, tile * LANES), min(last, (tile + 1) * LANES)
                    if lo < hi:
                        lane = (tile * rows_y + y) * size
                        field_refs[chunk * rows_y + y][lo - first : hi - first, lanes] = turned[
                            lo - tile * LANES : hi - tile * LANES, lane : lane + size
                        ]
            for k, z in enumerate(singles):
                tile, row = divmod(z, LANES)
                lane = (tile * rows_y + y) * size
                ref, at = (edge_ref, k * rows_y + y) if k < 2 else (inner_ref, (k - 2) * rows_y + y)
                ref[at : at + 1, lanes] = turned[row : row + 1, lane : lane + size]


def prepare(phi, pot, cuts):
    groups, block, rows_y, rows_z = phi.shape
    tiles = rows_z // LANES
    flat = (
        phi.reshape(groups, block, rows_y, tiles, LANES)
        .transpose(0, 1, 3, 2, 4)
        .reshape(groups * block * tiles * rows_y, LANES)
    )
    parts = tiles * rows_y
    per_step = 8
    width = per_step * block
    chunks = len(cuts) - 1
    spans = [last - first for first, last in zip(cuts, cuts[1:])]
    sizes = [span for span in spans for _ in range(rows_y)] + [2 * rows_y, 2 * rows_y * max(1, chunks - 1)]
    outs = pl.pallas_call(
        functools.partial(prepare_kernel, per_step, cuts, rows_y, tiles),
        grid=(groups // per_step,),
        in_specs=[
            pl.BlockSpec((per_step * block * parts, LANES), lambda s: (s, 0)),
            pl.BlockSpec((block * parts, block * parts), lambda s: (0, 0)),
            pl.BlockSpec((groups, rows_y, rows_z), lambda s: (0, 0, 0)),
        ],
        out_specs=[pl.BlockSpec((size, width), lambda s: (0, s)) for size in sizes]
        + [pl.BlockSpec((rows_y * span, groups), lambda s: (0, 0)) for span in spans],
        out_shape=[jax.ShapeDtypeStruct((size, groups * block), jnp.bfloat16) for size in sizes]
        + [jax.ShapeDtypeStruct((rows_y * span, groups), jnp.float32) for span in spans],
        compiler_params=pltpu.CompilerParams(vmem_limit_bytes=2 * SCOPED),
        name="prepare",
    )(*in_hbm(flat, regroup_matrix(block, parts), pot))
    fields = [[outs[c * rows_y + y] for y in range(rows_y)] for c in range(chunks)]
    return fields, outs[chunks * rows_y], outs[chunks * rows_y + 1], outs[chunks * rows_y + 2 :]


def stacked_blocks(ref, which_ref, pair, groups):
    return jnp.concatenate(
        [
            jnp.concatenate([ref[which_ref[(2 * pair + j) * groups + row]] for j in range(2)], axis=1)
            for row in range(groups)
        ],
        axis=0,
    )


def phi_kernel(groups, rows_y, loads, which_ref, *refs):
    y_refs, refs = refs[:rows_y], refs[rows_y:]
    if loads:
        (kern_hbm, hk_hbm), (rows_ref, sum_ref, kern_ref, hk_ref, sems) = refs[:2], refs[2:]
    else:
        hk_ref, rows_ref, sum_ref = refs
    zc = y_refs[0].shape[0]
    pair = pl.program_id(0)

    def copies():
        count = kern_hbm.shape[0]
        return [
            pltpu.make_async_copy(source, target.at[:count], sems.at[k])
            for k, (source, target) in enumerate(((hk_hbm, hk_ref), (kern_hbm, kern_ref)))
        ]

    @pl.when(pair == 0)
    def _():
        if loads:
            for copy in copies():
                copy.start()
            for ref in (kern_ref, hk_ref):
                ref[ref.shape[0] - 1] = jnp.zeros(ref.shape[1:], ref.dtype)
        for y, ref in enumerate(y_refs):
            rows_ref[y * zc : (y + 1) * zc, :] = ref[...]
        if loads:
            copies()[0].wait()

    sum_ref[pair] = jnp.dot(
        rows_ref[...], stacked_blocks(hk_ref, which_ref, pair, groups), preferred_element_type=jnp.float32
    )
    if loads:

        @pl.when(pair == pl.num_programs(0) - 1)
        def _():
            copies()[1].wait()


def phi_part(fields, groups, which, kern_hk, kern=None):
    zc, width = fields[0].shape
    n = len(fields) * zc
    block = width // groups
    pairs = which.shape[0] // groups // 2
    loads = kern is not None
    hbm = pl.BlockSpec(memory_space=pltpu.HBM)
    out_shape = [pltpu.VMEM((n, width), jnp.bfloat16), pltpu.VMEM((pairs, n, 2 * block), jnp.float32)]
    if loads:
        out_shape += [pltpu.VMEM((part.shape[0] + 1, *part.shape[1:]), part.dtype) for part in (kern, kern_hk)]
    return pl.pallas_call(
        functools.partial(phi_kernel, groups, len(fields), loads),
        grid_spec=pltpu.PrefetchScalarGridSpec(
            num_scalar_prefetch=1,
            grid=(pairs,),
            in_specs=[VMEM] * len(fields) + ([hbm] * 2 if loads else [VMEM]),
            out_specs=[VMEM] * len(out_shape),
            scratch_shapes=[pltpu.SemaphoreType.DMA((2,))] if loads else [],
        ),
        out_shape=out_shape,
        compiler_params=pltpu.CompilerParams(vmem_limit_bytes=SCOPED),
        cost_estimate=pl.CostEstimate(
            flops=hinted(4 * n * width * pairs * block), transcendentals=0, bytes_accessed=2 * n * width
        ),
        name="phi_part",
    )(which, *fields, *(in_hbm(kern, kern_hk) if loads else [kern_hk]))


def fill_action(rows_y, groups, act_ref, rows, prev_ref, next_ref, low_ref, high_ref, low_at, high_at, flags, pot_ref, mix_ref):
    depth = act_ref.shape[1]
    zc = act_ref.shape[0] // rows_y
    block = depth // groups
    wide = 4
    scales = [0.5 if flag is None else 0.5 * flag.astype(jnp.float32) for flag in flags]
    for first in range(0, groups, wide):
        lanes = slice(first * block, (first + wide) * block)
        around = jnp.concatenate([prev_ref[:, lanes], rows[:, lanes], next_ref[:, lanes]], axis=0)
        beside = jnp.dot(mix_ref[...], around, preferred_element_type=jnp.float32)
        for y in range(rows_y):
            at = slice(y * zc, (y + 1) * zc)
            field = rows[at, lanes]
            pots = jnp.concatenate(
                [jnp.broadcast_to(pot_ref[at, row : row + 1], (zc, block)) for row in range(first, first + wide)],
                axis=1,
            )
            value = beside[at] - pots * field.astype(jnp.float32)
            low = scales[0] * low_ref[low_at + y : low_at + y + 1, lanes].astype(jnp.float32)
            high = scales[1] * high_ref[high_at + y : high_at + y + 1, lanes].astype(jnp.float32)
            z = lax.broadcasted_iota(jnp.int32, (8, wide * block), 0)
            head = value[:8] + jnp.where(z == 0, low, 0.0)
            tail = value[zc - 8 :] + jnp.where(z == 7, high, 0.0)
            act_ref[at, lanes] = jnp.concatenate([head, value[8 : zc - 8], tail], axis=0).astype(jnp.bfloat16)


def action_kernel(groups, rows_y, cols, low_at, high_at, masked, which_ref, *refs):
    rows_ref, sum_ref, prev_ref, next_ref, low_ref, high_ref, pot_ref, mix_ref, kern_ref, act_ref = refs[:10]
    outs = refs[10:]
    pair = pl.program_id(0)
    n = rows_ref.shape[0]
    extra = cols * groups

    @pl.when(pair == 0)
    def _():
        flags = [which_ref[extra + k] if masked[k] else None for k in range(2)]
        fill_action(
            rows_y, groups, act_ref, rows_ref, prev_ref, next_ref, low_ref, high_ref, low_at, high_at, flags, pot_ref, mix_ref
        )
        if len(outs) == 2:
            code = jnp.full((16, outs[0].shape[1]), which_ref[extra + 2].astype(jnp.float32)).astype(jnp.bfloat16)
            for ref in outs:
                ref[ref.shape[0] - 16 :, :] = code

    value = sum_ref[pair] + jnp.dot(
        act_ref[...], stacked_blocks(kern_ref, which_ref, pair, groups), preferred_element_type=jnp.float32
    )
    block = value.shape[1] // 2
    split = cols // 2 // len(outs)

    def store(ref, first):
        for j in range(2):
            at = pl.multiple_of((2 * (pair - first) + j) * n, 16)
            ref[pl.ds(at, n), :] = value[:, j * block : (j + 1) * block].astype(jnp.bfloat16)

    if len(outs) == 1:
        store(outs[0], 0)
    else:

        @pl.when(pair < split)
        def _():
            store(outs[0], 0)

        @pl.when(pair >= split)
        def _():
            store(outs[1], split)


def action_part(rows, partial, prev, below, low, low_at, high, high_at, masked, pot, groups, rows_y, cols, which, kern, halves):
    n, width = rows.shape
    zc = n // rows_y
    block = width // groups
    out_rows = [cols // halves * n + (16 if halves == 2 else 0)] * halves
    return pl.pallas_call(
        functools.partial(action_kernel, groups, rows_y, cols, low_at, high_at, masked),
        grid_spec=pltpu.PrefetchScalarGridSpec(
            num_scalar_prefetch=1,
            grid=(cols // 2,),
            in_specs=[VMEM] * 9,
            out_specs=[VMEM] * (1 + halves),
        ),
        out_shape=[pltpu.VMEM((n, width), jnp.bfloat16)]
        + [pltpu.VMEM((rows_out, block), jnp.bfloat16) for rows_out in out_rows],
        compiler_params=pltpu.CompilerParams(vmem_limit_bytes=SCOPED),
        cost_estimate=pl.CostEstimate(
            flops=hinted(2 * n * width * cols * block), transcendentals=0, bytes_accessed=2 * n * width
        ),
        name="action_part",
    )(which, rows, partial, prev, below, low, high, pot, stencil_matrix(zc, rows_y), kern)


def onward_kernel(away_ref, q0_ref, q1_ref, right_ref, right_code, left_ref, left_code, to_right, to_left):
    for mine, direction, arrived, code, out in (
        (q1_ref, RIGHT, right_ref, right_code, to_right),
        (q0_ref, LEFT, left_ref, left_code, to_left),
    ):
        kept = jnp.where(away_ref[0] == direction, mine[...].astype(jnp.float32), 0.0)
        through = code[:1, :].astype(jnp.float32) == ACROSS
        out[...] = (kept + jnp.where(through, arrived[...].astype(jnp.float32), 0.0)).astype(jnp.bfloat16)


def send_onward(away, q0, q1, right1, left1):
    rows, block = q0.shape
    steps = 4
    size = (rows - 16) // steps
    part = pl.BlockSpec((size, block), lambda s, a: (s, 0))
    code = pl.BlockSpec((16, block), lambda s, a: ((rows - 16) // 16, 0))
    return pl.pallas_call(
        onward_kernel,
        grid_spec=pltpu.PrefetchScalarGridSpec(
            num_scalar_prefetch=1,
            grid=(steps,),
            in_specs=[part, part, part, code, part, code],
            out_specs=[part, part],
        ),
        out_shape=[jax.ShapeDtypeStruct((rows - 16, block), jnp.bfloat16)] * 2,
        compiler_params=pltpu.CompilerParams(vmem_limit_bytes=SCOPED),
        cost_estimate=pl.CostEstimate(flops=0, transcendentals=0, bytes_accessed=12 * rows * block),
        name="send_onward",
    )(away, q0, q1, right1, right1, left1, left1)


def local_kernel(groups, which_ref, act_ref, rows_ref, kern_ref, hk_ref, left_ref, left_code, right_ref, right_code, out_ref):
    pair = pl.program_id(0)
    value = jnp.dot(
        act_ref[...], stacked_blocks(kern_ref, which_ref, pair, groups), preferred_element_type=jnp.float32
    ) + jnp.dot(rows_ref[...], stacked_blocks(hk_ref, which_ref, pair, groups), preferred_element_type=jnp.float32)
    n = rows_ref.shape[0]
    block = value.shape[1] // 2

    def store(arrived, code, wanted):
        mine = code[:1, :].astype(jnp.float32) == wanted
        for j in range(2):
            at = slice(j * n, (j + 1) * n)
            more = jnp.where(mine, arrived[at, :].astype(jnp.float32), 0.0)
            out_ref[at, :] = (value[:, j * block : (j + 1) * block] + more).astype(jnp.bfloat16)

    half = pl.num_programs(0) // 2

    @pl.when(pair < half)
    def _():
        store(left_ref, left_code, LEFT)

    @pl.when(pair >= half)
    def _():
        store(right_ref, right_code, RIGHT)


def local_columns(act, rows, groups, which, kern, kern_hk, left1, right1):
    cols = which.shape[0] // groups
    n, width = rows.shape
    block = width // groups
    half = cols // 4
    code = pl.BlockSpec((16, block), lambda p, w: (cols // 2 * n // 16, 0))
    return pl.pallas_call(
        functools.partial(local_kernel, groups),
        grid_spec=pltpu.PrefetchScalarGridSpec(
            num_scalar_prefetch=1,
            grid=(cols // 2,),
            in_specs=[VMEM] * 4
            + [pl.BlockSpec((2 * n, block), lambda p, w: (jnp.minimum(p, half - 1), 0)), code]
            + [pl.BlockSpec((2 * n, block), lambda p, w: (jnp.maximum(p - half, 0), 0)), code],
            out_specs=pl.BlockSpec((2 * n, block), lambda p, w: (p, 0)),
        ),
        out_shape=jax.ShapeDtypeStruct((cols * n, block), jnp.bfloat16),
        compiler_params=pltpu.CompilerParams(vmem_limit_bytes=SCOPED),
        cost_estimate=pl.CostEstimate(
            flops=hinted(4 * n * width * cols * block), transcendentals=0, bytes_accessed=2 * n * width
        ),
        name="local_columns",
    )(which, act, rows, kern, kern_hk, left1, left1, right1, right1)


def write_columns(rows_y, tiles, columns, mix_ref, out_ref):
    sizes = [value.shape[0] // rows_y for value in columns[0]]
    rows = mix_ref.shape[0]
    turned = []
    for values in columns:
        parts = []
        for tile in range(tiles):
            for y in range(rows_y):
                pieces = []
                for chunk, zc in enumerate(sizes):
                    first = sum(sizes[:chunk])
                    lo, hi = max(first, tile * LANES), min(first + zc, (tile + 1) * LANES)
                    if lo < hi:
                        pieces.append(values[chunk][y * zc + lo - first : y * zc + hi - first, :])
                part = jnp.concatenate(pieces, axis=0) if len(pieces) > 1 else pieces[0]
                parts.append((-2.0 * part).astype(jnp.bfloat16))
        turned.append(jnp.concatenate(parts, axis=1))
    wide = 2
    for first in range(0, len(turned), wide):
        both = jnp.concatenate(turned[first : first + wide], axis=0)
        out = lax.dot_general(mix_ref[...], both, (((1,), (1,)), ((), ())), preferred_element_type=jnp.float32)
        for j in range(wide):
            out_ref[(first + j) * rows : (first + j + 1) * rows, :] = out[:, j * LANES : (j + 1) * LANES].astype(
                jnp.bfloat16
            )


def final_kernel(per_step, counts, rows_y, tiles, mix_ref, *refs):
    out_ref = refs[-1]
    columns = []
    for col in range(per_step):
        values, first = [], 0
        for count in counts:
            n = refs[first].shape[0] // per_step
            at = slice(col * n, (col + 1) * n)
            values.append(sum(ref[at, :].astype(jnp.float32) for ref in refs[first : first + count]))
            first += count
        columns.append(values)
    write_columns(rows_y, tiles, columns, mix_ref, out_ref)


def finish(parts, firsts, cols, all_cols, rows_y, rows_z, before=None):
    arrays = [array for part in parts for array in part]
    block = arrays[0].shape[1]
    tiles = rows_z // LANES
    rows = block * tiles * rows_y
    per_step = 4
    start = firsts[0] // per_step
    in_specs = [pl.BlockSpec((rows, rows), lambda s: (0, 0))]
    for part in parts:
        n = part[0].shape[0] // all_cols
        for first, _ in zip(firsts, part):
            in_specs.append(
                pl.BlockSpec((per_step * n, block), functools.partial(lambda at, s: (s + at, 0), first // per_step))
            )
    arrays = [*in_hbm(regroup_matrix(block, tiles * rows_y)), *arrays]
    counts = [len(part) for part in parts]
    kernel = functools.partial(final_kernel, per_step, counts, rows_y, tiles)
    aliases = {}
    if before is not None:
        aliases = {len(arrays): 0}
        arrays.append(before)
        in_specs.append(pl.BlockSpec(memory_space=pl.ANY))
        kernel = lambda *refs: final_kernel(per_step, counts, rows_y, tiles, *refs[:-2], refs[-1])
    return pl.pallas_call(
        kernel,
        grid=(cols // per_step,),
        in_specs=in_specs,
        out_specs=pl.BlockSpec((per_step * rows, LANES), lambda s: (s + start, 0)),
        out_shape=jax.ShapeDtypeStruct((all_cols * rows, LANES), jnp.bfloat16),
        input_output_aliases=aliases,
        compiler_params=pltpu.CompilerParams(vmem_limit_bytes=SCOPED),
        name="finish",
    )(*arrays)


def unflatten(flat, cols, block, rows_y, tiles):
    return (
        flat.reshape(cols, block, tiles, rows_y, LANES)
        .transpose(0, 1, 3, 2, 4)
        .reshape(cols, block, rows_y, tiles * LANES)
    )


def block_of_column(slot_of, slots):
    hit = slot_of[None, :, :] == slots[:, None, None]
    zero = slot_of.size
    place = jnp.arange(zero, dtype=jnp.int32).reshape(slot_of.shape) - zero
    return zero + jnp.sum(jnp.where(hit, place, 0), axis=2)


def shifts(axis, by):
    count = lax.axis_size(axis)
    return [(i, i + by) for i in range(count) if 0 <= i + by < count]


def outer_rows(edges, rows_y):
    if lax.axis_size("gz") == 2:
        return lax.ppermute(edges, "gz", [(0, 1), (1, 0)])
    after_last = lax.ppermute(edges[:rows_y], "gz", shifts("gz", -1))
    before_first = lax.ppermute(edges[rows_y:], "gz", shifts("gz", 1))
    return jnp.concatenate([after_last, before_first], axis=0)


def per_device(phi, pot, kern, kern_hk, slot_of, req_cols):
    groups, block, rows_y, rows_z = phi.shape
    listed = req_cols.shape[0]
    ring = lax.axis_size("gx")
    cuts = CUTS if CUTS[-1] == rows_z else (0, rows_z)
    chunks = len(cuts) - 1

    fields, edges, inner, pots = prepare(phi, pot, cuts)
    halo = []

    def send_halo(c, *before):
        up, down = after(fields[c][-1], *before), after(fields[c][0], *before)
        halo.append((lax.ppermute(up, "gy", shifts("gy", 1)), lax.ppermute(down, "gy", shifts("gy", -1))))

    send_halo(0)
    outer = outer_rows(edges, rows_y)
    req_cols, slot_of, _ = lax.optimization_barrier((req_cols, slot_of, edges))
    kern = kern.reshape(-1, block, block)
    kern_hk = kern_hk.reshape(-1, block, block)
    place = lax.axis_index("gz")
    marks = [place > 0, place < lax.axis_size("gz") - 1]

    def sides(c):
        low = (outer, rows_y) if c == 0 else (inner, (2 * c - 2) * rows_y)
        high = (outer, 0) if c == chunks - 1 else (inner, (2 * c + 1) * rows_y)
        return *low, *high, (c == 0, c == chunks - 1)

    blocks = []

    def phi_columns(c, names):
        if blocks:
            return phi_part(fields[c], groups, names, blocks[1])
        mine, partial, *loaded = phi_part(fields[c], groups, names, kern_hk, kern)
        blocks.extend(loaded)
        return mine, partial

    def all_columns(c, mine, partial, table, cols, halves):
        return action_part(
            mine, partial, *halo[c], *sides(c), pots[c], groups, rows_y, cols, table, blocks[0], halves
        )

    if ring != 4:
        which = block_of_column(slot_of, jnp.arange(listed, dtype=jnp.int32)).reshape(-1)
        table = jnp.concatenate([which, jnp.stack(marks).astype(jnp.int32)])
        hit = req_cols[None, :] == jnp.arange(groups * ring, dtype=jnp.int32)[:, None]
        named = jnp.any(hit, axis=1)
        source = jnp.sum(jnp.where(hit, jnp.arange(listed, dtype=jnp.int32), 0), axis=1)
        parts = []
        for c in range(chunks):
            if c:
                send_halo(c, table)
            _, sums = all_columns(c, *phi_columns(c, which), table, listed, 1)
            spread = jnp.where(named[:, None, None], sums.reshape(listed, -1, block)[source], 0)
            total = lax.psum_scatter(spread, "gx", scatter_dimension=0, tiled=True)
            parts.append([total.reshape(-1, block)])
        flat = finish(parts, (0,), groups, groups, rows_y, rows_z)
        return unflatten(flat, groups, block, rows_y, rows_z // LANES)

    me = lax.axis_index("gx")
    toward = (req_cols // groups - me) % ring
    away = jnp.max(toward)
    ahead = [(i, (i + 1) % ring) for i in range(ring)]
    behind = [(i, (i - 1) % ring) for i in range(ring)]

    half = groups // 2
    column = req_cols % groups
    first = jnp.where(toward == ACROSS, column, (column + half) % groups)
    order = jnp.where(toward == 0, groups + column, first)
    slots = jnp.sum(
        jnp.where(
            jnp.arange(2 * groups, dtype=jnp.int32)[:, None] == order[None, :], jnp.arange(listed, dtype=jnp.int32), 0
        ),
        axis=1,
    )
    which = block_of_column(slot_of, slots).reshape(-1)
    far, near = which[: groups * groups], which[groups * groups :]
    table = jnp.concatenate([far, jnp.stack([*marks, away]).astype(jnp.int32)])
    away = away.reshape(1)
    send_halo(1, far)

    rows, acts, sent, own, right1, left1, right2, left2 = [], [], [], [], [], [], [], []

    def send_first(c, *before):
        mine, partial = phi_columns(c, after(far, *before))
        act, q0, q1 = all_columns(c, mine, partial, after(table, *before), groups, 2)
        rows.append(mine)
        acts.append(act)
        sent.append((q0, q1))
        right1.append(lax.ppermute(q0, "gx", ahead))
        left1.append(lax.ppermute(q1, "gx", behind))

    def send_second(c, *before):
        arrived = lax.optimization_barrier((right1[c], left1[c], *before))
        right1[c], left1[c] = arrived[:2]
        to_right, to_left = send_onward(away, *sent[c], right1[c], left1[c])
        right2.append(lax.ppermute(to_right, "gx", ahead))
        left2.append(lax.ppermute(to_left, "gx", behind))
        own.append(
            local_columns(acts[c], rows[c], groups, after(near, to_right, *right2[:c], *left2[:c]), *blocks, left1[c], right1[c])
        )

    send_first(0)
    for c in range(1, chunks):
        if c + 1 < chunks:
            send_halo(c + 1, sent[c - 1][1])
        send_first(c, *sent[c - 1])
        send_second(c - 1, *sent[c])
    send_second(chunks - 1, own[-1])
    flat = finish(list(zip(own, right2)), (0, 0), half, groups, rows_y, rows_z)
    left2 = lax.optimization_barrier((*left2, flat))
    flat = finish(list(zip(own, left2)), (half, 0), half, groups, rows_y, rows_z, left2[-1])
    return unflatten(flat, groups, block, rows_y, rows_z // LANES)


def solution(mesh):
    placed = (
        P("gx", None, "gy", "gz"),
        P("gx", "gy", "gz"),
        P("gx", None, None, None),
        P("gx", None, None, None),
        P("gx", None),
        P("gx"),
    )
    return jax.shard_map(
        per_device, mesh=mesh, in_specs=placed, out_specs=P("gx", None, "gy", "gz"), check_vma=False
    )
```

```python
import functools

import jax
import jax.numpy as jnp
import numpy as np
from jax import lax
from jax.experimental import pallas as pl
from jax.experimental.pallas import tpu as pltpu
from jax.sharding import PartitionSpec as P

CUTS = (0, 96, 176, 256)
RIGHT, ACROSS, LEFT = 1, 2, 3
LANES = 128
SCOPED = 8 << 20
VMEM = pl.BlockSpec(memory_space=pltpu.VMEM)


def hinted(flops):
    return flops // 4


def in_hbm(*arrays):
    return [pltpu.with_memory_space_constraint(array, pltpu.HBM) for array in arrays]


def after(value, *before):
    return lax.optimization_barrier((value, *before))[0]


def regroup_matrix(block, parts):
    rows = np.arange(block * parts)
    out = np.zeros((block * parts, block * parts), np.float32)
    out[rows, (rows % parts) * block + rows // parts] = 1.0
    return jnp.asarray(out, jnp.bfloat16)


def stencil_matrix(zc, rows_y):
    out = np.zeros((rows_y, zc, rows_y + 2, zc), np.float32)
    z = np.arange(zc)
    for y in range(rows_y):
        out[y, z, y, z] = 0.5
        out[y, z, y + 2, z] = 0.5
        out[y, z, y + 1, z] = -2.0
        out[y, z[1:], y + 1, z[:-1]] = 0.5
        out[y, z[:-1], y + 1, z[1:]] = 0.5
    return jnp.asarray(out.reshape(rows_y * zc, (rows_y + 2) * zc), jnp.bfloat16)


def prepare_kernel(per_step, cuts, rows_y, tiles, phi_ref, mix_ref, pot_ref, *out_refs):
    block = mix_ref.shape[0]
    size = block // (tiles * rows_y)
    spans = list(zip(cuts, cuts[1:]))
    singles = [0, cuts[-1] - 1] + [z for cut in cuts[1:-1] for z in (cut - 1, cut)]
    field_refs = out_refs[: len(spans) * rows_y]
    edge_ref, inner_ref = out_refs[len(spans) * rows_y : len(spans) * rows_y + 2]
    turned_pot_refs = out_refs[len(spans) * rows_y + 2 :]

    @pl.when(pl.program_id(0) == 0)
    def _():
        for y in range(rows_y):
            turned = pot_ref[:, y, :].T
            for ref, (first, last) in zip(turned_pot_refs, spans):
                ref[y * (last - first) : (y + 1) * (last - first), :] = turned[first:last]

    for step in range(per_step):
        part = phi_ref[step * block : (step + 1) * block, :]
        turned = lax.dot_general(
            part, mix_ref[...], (((0,), (0,)), ((), ())), preferred_element_type=jnp.float32
        ).astype(jnp.bfloat16)
        lanes = slice(step * size, (step + 1) * size)
        for y in range(rows_y):
            for chunk, (first, last) in enumerate(spans):
                for tile in range(tiles):
                    lo, hi = max(first, tile * LANES), min(last, (tile + 1) * LANES)
                    if lo < hi:
                        lane = (tile * rows_y + y) * size
                        field_refs[chunk * rows_y + y][lo - first : hi - first, lanes] = turned[
                            lo - tile * LANES : hi - tile * LANES, lane : lane + size
                        ]
            for k, z in enumerate(singles):
                tile, row = divmod(z, LANES)
                lane = (tile * rows_y + y) * size
                ref, at = (edge_ref, k * rows_y + y) if k < 2 else (inner_ref, (k - 2) * rows_y + y)
                ref[at : at + 1, lanes] = turned[row : row + 1, lane : lane + size]


def prepare(phi, pot, cuts):
    groups, block, rows_y, rows_z = phi.shape
    tiles = rows_z // LANES
    flat = (
        phi.reshape(groups, block, rows_y, tiles, LANES)
        .transpose(0, 1, 3, 2, 4)
        .reshape(groups * block * tiles * rows_y, LANES)
    )
    parts = tiles * rows_y
    per_step = 8
    width = per_step * block
    chunks = len(cuts) - 1
    spans = [last - first for first, last in zip(cuts, cuts[1:])]
    sizes = [span for span in spans for _ in range(rows_y)] + [2 * rows_y, 2 * rows_y * max(1, chunks - 1)]
    outs = pl.pallas_call(
        functools.partial(prepare_kernel, per_step, cuts, rows_y, tiles),
        grid=(groups // per_step,),
        in_specs=[
            pl.BlockSpec((per_step * block * parts, LANES), lambda s: (s, 0)),
            pl.BlockSpec((block * parts, block * parts), lambda s: (0, 0)),
            pl.BlockSpec((groups, rows_y, rows_z), lambda s: (0, 0, 0)),
        ],
        out_specs=[pl.BlockSpec((size, width), lambda s: (0, s)) for size in sizes]
        + [pl.BlockSpec((rows_y * span, groups), lambda s: (0, 0)) for span in spans],
        out_shape=[jax.ShapeDtypeStruct((size, groups * block), jnp.bfloat16) for size in sizes]
        + [jax.ShapeDtypeStruct((rows_y * span, groups), jnp.float32) for span in spans],
        compiler_params=pltpu.CompilerParams(vmem_limit_bytes=2 * SCOPED),
        name="prepare",
    )(*in_hbm(flat, regroup_matrix(block, parts), pot))
    fields = [[outs[c * rows_y + y] for y in range(rows_y)] for c in range(chunks)]
    return fields, outs[chunks * rows_y], outs[chunks * rows_y + 1], outs[chunks * rows_y + 2 :]


def stacked_blocks(ref, which_ref, pair, groups):
    return jnp.concatenate(
        [
            jnp.concatenate([ref[which_ref[(2 * pair + j) * groups + row]] for j in range(2)], axis=1)
            for row in range(groups)
        ],
        axis=0,
    )


def phi_kernel(groups, rows_y, loads, which_ref, *refs):
    y_refs, refs = refs[:rows_y], refs[rows_y:]
    if loads:
        (kern_hbm, hk_hbm), (rows_ref, sum_ref, kern_ref, hk_ref, sems) = refs[:2], refs[2:]
    else:
        hk_ref, rows_ref, sum_ref = refs
    zc = y_refs[0].shape[0]
    pair = pl.program_id(0)

    def copies():
        count = kern_hbm.shape[0]
        return [
            pltpu.make_async_copy(source, target.at[:count], sems.at[k])
            for k, (source, target) in enumerate(((hk_hbm, hk_ref), (kern_hbm, kern_ref)))
        ]

    @pl.when(pair == 0)
    def _():
        if loads:
            for copy in copies():
                copy.start()
            for ref in (kern_ref, hk_ref):
                ref[ref.shape[0] - 1] = jnp.zeros(ref.shape[1:], ref.dtype)
        for y, ref in enumerate(y_refs):
            rows_ref[y * zc : (y + 1) * zc, :] = ref[...]
        if loads:
            copies()[0].wait()

    sum_ref[pair] = jnp.dot(
        rows_ref[...], stacked_blocks(hk_ref, which_ref, pair, groups), preferred_element_type=jnp.float32
    )
    if loads:

        @pl.when(pair == pl.num_programs(0) - 1)
        def _():
            copies()[1].wait()


def phi_part(fields, groups, which, kern_hk, kern=None):
    zc, width = fields[0].shape
    n = len(fields) * zc
    block = width // groups
    pairs = which.shape[0] // groups // 2
    loads = kern is not None
    hbm = pl.BlockSpec(memory_space=pltpu.HBM)
    out_shape = [pltpu.VMEM((n, width), jnp.bfloat16), pltpu.VMEM((pairs, n, 2 * block), jnp.float32)]
    if loads:
        out_shape += [pltpu.VMEM((part.shape[0] + 1, *part.shape[1:]), part.dtype) for part in (kern, kern_hk)]
    return pl.pallas_call(
        functools.partial(phi_kernel, groups, len(fields), loads),
        grid_spec=pltpu.PrefetchScalarGridSpec(
            num_scalar_prefetch=1,
            grid=(pairs,),
            in_specs=[VMEM] * len(fields) + ([hbm] * 2 if loads else [VMEM]),
            out_specs=[VMEM] * len(out_shape),
            scratch_shapes=[pltpu.SemaphoreType.DMA((2,))] if loads else [],
        ),
        out_shape=out_shape,
        compiler_params=pltpu.CompilerParams(vmem_limit_bytes=SCOPED),
        cost_estimate=pl.CostEstimate(
            flops=hinted(4 * n * width * pairs * block), transcendentals=0, bytes_accessed=2 * n * width
        ),
        name="phi_part",
    )(which, *fields, *(in_hbm(kern, kern_hk) if loads else [kern_hk]))


def fill_action(rows_y, groups, act_ref, rows, prev_ref, next_ref, low_ref, high_ref, low_at, high_at, flags, pot_ref, mix_ref):
    depth = act_ref.shape[1]
    zc = act_ref.shape[0] // rows_y
    block = depth // groups
    wide = 4
    scales = [0.5 if flag is None else 0.5 * flag.astype(jnp.float32) for flag in flags]
    for first in range(0, groups, wide):
        lanes = slice(first * block, (first + wide) * block)
        around = jnp.concatenate([prev_ref[:, lanes], rows[:, lanes], next_ref[:, lanes]], axis=0)
        beside = jnp.dot(mix_ref[...], around, preferred_element_type=jnp.float32)
        for y in range(rows_y):
            at = slice(y * zc, (y + 1) * zc)
            field = rows[at, lanes]
            pots = jnp.concatenate(
                [jnp.broadcast_to(pot_ref[at, row : row + 1], (zc, block)) for row in range(first, first + wide)],
                axis=1,
            )
            value = beside[at] - pots * field.astype(jnp.float32)
            low = scales[0] * low_ref[low_at + y : low_at + y + 1, lanes].astype(jnp.float32)
            high = scales[1] * high_ref[high_at + y : high_at + y + 1, lanes].astype(jnp.float32)
            z = lax.broadcasted_iota(jnp.int32, (8, wide * block), 0)
            head = value[:8] + jnp.where(z == 0, low, 0.0)
            tail = value[zc - 8 :] + jnp.where(z == 7, high, 0.0)
            act_ref[at, lanes] = jnp.concatenate([head, value[8 : zc - 8], tail], axis=0).astype(jnp.bfloat16)


def action_kernel(groups, rows_y, cols, low_at, high_at, masked, which_ref, *refs):
    rows_ref, sum_ref, prev_ref, next_ref, low_ref, high_ref, pot_ref, mix_ref, kern_ref, act_ref = refs[:10]
    outs = refs[10:]
    pair = pl.program_id(0)
    n = rows_ref.shape[0]
    extra = cols * groups

    @pl.when(pair == 0)
    def _():
        flags = [which_ref[extra + k] if masked[k] else None for k in range(2)]
        fill_action(
            rows_y, groups, act_ref, rows_ref, prev_ref, next_ref, low_ref, high_ref, low_at, high_at, flags, pot_ref, mix_ref
        )
        if len(outs) == 2:
            code = jnp.full((16, outs[0].shape[1]), which_ref[extra + 2].astype(jnp.float32)).astype(jnp.bfloat16)
            for ref in outs:
                ref[ref.shape[0] - 16 :, :] = code

    value = sum_ref[pair] + jnp.dot(
        act_ref[...], stacked_blocks(kern_ref, which_ref, pair, groups), preferred_element_type=jnp.float32
    )
    block = value.shape[1] // 2
    split = cols // 2 // len(outs)

    def store(ref, first):
        for j in range(2):
            at = pl.multiple_of((2 * (pair - first) + j) * n, 16)
            ref[pl.ds(at, n), :] = value[:, j * block : (j + 1) * block].astype(jnp.bfloat16)

    if len(outs) == 1:
        store(outs[0], 0)
    else:

        @pl.when(pair < split)
        def _():
            store(outs[0], 0)

        @pl.when(pair >= split)
        def _():
            store(outs[1], split)


def action_part(rows, partial, prev, below, low, low_at, high, high_at, masked, pot, groups, rows_y, cols, which, kern, halves):
    n, width = rows.shape
    zc = n // rows_y
    block = width // groups
    out_rows = [cols // halves * n + (16 if halves == 2 else 0)] * halves
    return pl.pallas_call(
        functools.partial(action_kernel, groups, rows_y, cols, low_at, high_at, masked),
        grid_spec=pltpu.PrefetchScalarGridSpec(
            num_scalar_prefetch=1,
            grid=(cols // 2,),
            in_specs=[VMEM] * 9,
            out_specs=[VMEM] * (1 + halves),
        ),
        out_shape=[pltpu.VMEM((n, width), jnp.bfloat16)]
        + [pltpu.VMEM((rows_out, block), jnp.bfloat16) for rows_out in out_rows],
        compiler_params=pltpu.CompilerParams(vmem_limit_bytes=SCOPED),
        cost_estimate=pl.CostEstimate(
            flops=hinted(2 * n * width * cols * block), transcendentals=0, bytes_accessed=2 * n * width
        ),
        name="action_part",
    )(which, rows, partial, prev, below, low, high, pot, stencil_matrix(zc, rows_y), kern)


def onward_kernel(away_ref, q0_ref, q1_ref, right_ref, right_code, left_ref, left_code, to_right, to_left):
    for mine, direction, arrived, code, out in (
        (q1_ref, RIGHT, right_ref, right_code, to_right),
        (q0_ref, LEFT, left_ref, left_code, to_left),
    ):
        kept = jnp.where(away_ref[0] == direction, mine[...].astype(jnp.float32), 0.0)
        through = code[:1, :].astype(jnp.float32) == ACROSS
        out[...] = (kept + jnp.where(through, arrived[...].astype(jnp.float32), 0.0)).astype(jnp.bfloat16)


def send_onward(away, q0, q1, right1, left1):
    rows, block = q0.shape
    steps = 2
    size = (rows - 16) // steps
    part = pl.BlockSpec((size, block), lambda s, a: (s, 0))
    code = pl.BlockSpec((16, block), lambda s, a: ((rows - 16) // 16, 0))
    return pl.pallas_call(
        onward_kernel,
        grid_spec=pltpu.PrefetchScalarGridSpec(
            num_scalar_prefetch=1,
            grid=(steps,),
            in_specs=[part, part, part, code, part, code],
            out_specs=[part, part],
        ),
        out_shape=[jax.ShapeDtypeStruct((rows - 16, block), jnp.bfloat16)] * 2,
        compiler_params=pltpu.CompilerParams(vmem_limit_bytes=SCOPED),
        cost_estimate=pl.CostEstimate(flops=0, transcendentals=0, bytes_accessed=12 * rows * block),
        name="send_onward",
    )(away, q0, q1, right1, right1, left1, left1)


def local_kernel(groups, which_ref, act_ref, rows_ref, kern_ref, hk_ref, left_ref, left_code, right_ref, right_code, out_ref):
    pair = pl.program_id(0)
    value = jnp.dot(
        act_ref[...], stacked_blocks(kern_ref, which_ref, pair, groups), preferred_element_type=jnp.float32
    ) + jnp.dot(rows_ref[...], stacked_blocks(hk_ref, which_ref, pair, groups), preferred_element_type=jnp.float32)
    n = rows_ref.shape[0]
    block = value.shape[1] // 2

    def store(arrived, code, wanted):
        mine = code[:1, :].astype(jnp.float32) == wanted
        for j in range(2):
            at = slice(j * n, (j + 1) * n)
            more = jnp.where(mine, arrived[at, :].astype(jnp.float32), 0.0)
            out_ref[at, :] = (value[:, j * block : (j + 1) * block] + more).astype(jnp.bfloat16)

    half = pl.num_programs(0) // 2

    @pl.when(pair < half)
    def _():
        store(left_ref, left_code, LEFT)

    @pl.when(pair >= half)
    def _():
        store(right_ref, right_code, RIGHT)


def local_columns(act, rows, groups, which, kern, kern_hk, left1, right1):
    cols = which.shape[0] // groups
    n, width = rows.shape
    block = width // groups
    half = cols // 4
    code = pl.BlockSpec((16, block), lambda p, w: (cols // 2 * n // 16, 0))
    return pl.pallas_call(
        functools.partial(local_kernel, groups),
        grid_spec=pltpu.PrefetchScalarGridSpec(
            num_scalar_prefetch=1,
            grid=(cols // 2,),
            in_specs=[VMEM] * 4
            + [pl.BlockSpec((2 * n, block), lambda p, w: (jnp.minimum(p, half - 1), 0)), code]
            + [pl.BlockSpec((2 * n, block), lambda p, w: (jnp.maximum(p - half, 0), 0)), code],
            out_specs=pl.BlockSpec((2 * n, block), lambda p, w: (p, 0)),
        ),
        out_shape=jax.ShapeDtypeStruct((cols * n, block), jnp.bfloat16),
        compiler_params=pltpu.CompilerParams(vmem_limit_bytes=SCOPED),
        cost_estimate=pl.CostEstimate(
            flops=hinted(4 * n * width * cols * block), transcendentals=0, bytes_accessed=2 * n * width
        ),
        name="local_columns",
    )(which, act, rows, kern, kern_hk, left1, left1, right1, right1)


def write_columns(rows_y, tiles, columns, mix_ref, out_ref):
    sizes = [value.shape[0] // rows_y for value in columns[0]]
    rows = mix_ref.shape[0]
    turned = []
    for values in columns:
        parts = []
        for tile in range(tiles):
            for y in range(rows_y):
                pieces = []
                for chunk, zc in enumerate(sizes):
                    first = sum(sizes[:chunk])
                    lo, hi = max(first, tile * LANES), min(first + zc, (tile + 1) * LANES)
                    if lo < hi:
                        pieces.append(values[chunk][y * zc + lo - first : y * zc + hi - first, :])
                part = jnp.concatenate(pieces, axis=0) if len(pieces) > 1 else pieces[0]
                parts.append((-2.0 * part).astype(jnp.bfloat16))
        turned.append(jnp.concatenate(parts, axis=1))
    wide = 2
    for first in range(0, len(turned), wide):
        both = jnp.concatenate(turned[first : first + wide], axis=0)
        out = lax.dot_general(mix_ref[...], both, (((1,), (1,)), ((), ())), preferred_element_type=jnp.float32)
        for j in range(wide):
            out_ref[(first + j) * rows : (first + j + 1) * rows, :] = out[:, j * LANES : (j + 1) * LANES].astype(
                jnp.bfloat16
            )


def final_kernel(per_step, counts, rows_y, tiles, mix_ref, *refs):
    out_ref = refs[-1]
    columns = []
    for col in range(per_step):
        values, first = [], 0
        for count in counts:
            n = refs[first].shape[0] // per_step
            at = slice(col * n, (col + 1) * n)
            values.append(sum(ref[at, :].astype(jnp.float32) for ref in refs[first : first + count]))
            first += count
        columns.append(values)
    write_columns(rows_y, tiles, columns, mix_ref, out_ref)


def finish(parts, firsts, cols, all_cols, rows_y, rows_z, before=None):
    arrays = [array for part in parts for array in part]
    block = arrays[0].shape[1]
    tiles = rows_z // LANES
    rows = block * tiles * rows_y
    per_step = 4
    start = firsts[0] // per_step
    in_specs = [pl.BlockSpec((rows, rows), lambda s: (0, 0))]
    for part in parts:
        n = part[0].shape[0] // all_cols
        for first, _ in zip(firsts, part):
            in_specs.append(
                pl.BlockSpec((per_step * n, block), functools.partial(lambda at, s: (s + at, 0), first // per_step))
            )
    arrays = [*in_hbm(regroup_matrix(block, tiles * rows_y)), *arrays]
    counts = [len(part) for part in parts]
    kernel = functools.partial(final_kernel, per_step, counts, rows_y, tiles)
    aliases = {}
    if before is not None:
        aliases = {len(arrays): 0}
        arrays.append(before)
        in_specs.append(pl.BlockSpec(memory_space=pl.ANY))
        kernel = lambda *refs: final_kernel(per_step, counts, rows_y, tiles, *refs[:-2], refs[-1])
    return pl.pallas_call(
        kernel,
        grid=(cols // per_step,),
        in_specs=in_specs,
        out_specs=pl.BlockSpec((per_step * rows, LANES), lambda s: (s + start, 0)),
        out_shape=jax.ShapeDtypeStruct((all_cols * rows, LANES), jnp.bfloat16),
        input_output_aliases=aliases,
        compiler_params=pltpu.CompilerParams(vmem_limit_bytes=SCOPED),
        name="finish",
    )(*arrays)


def unflatten(flat, cols, block, rows_y, tiles):
    return (
        flat.reshape(cols, block, tiles, rows_y, LANES)
        .transpose(0, 1, 3, 2, 4)
        .reshape(cols, block, rows_y, tiles * LANES)
    )


def block_of_column(slot_of, slots):
    hit = slot_of[None, :, :] == slots[:, None, None]
    zero = slot_of.size
    place = jnp.arange(zero, dtype=jnp.int32).reshape(slot_of.shape) - zero
    return zero + jnp.sum(jnp.where(hit, place, 0), axis=2)


def shifts(axis, by):
    count = lax.axis_size(axis)
    return [(i, i + by) for i in range(count) if 0 <= i + by < count]


def outer_rows(edges, rows_y):
    if lax.axis_size("gz") == 2:
        return lax.ppermute(edges, "gz", [(0, 1), (1, 0)])
    after_last = lax.ppermute(edges[:rows_y], "gz", shifts("gz", -1))
    before_first = lax.ppermute(edges[rows_y:], "gz", shifts("gz", 1))
    return jnp.concatenate([after_last, before_first], axis=0)


def per_device(phi, pot, kern, kern_hk, slot_of, req_cols):
    groups, block, rows_y, rows_z = phi.shape
    listed = req_cols.shape[0]
    ring = lax.axis_size("gx")
    cuts = CUTS if CUTS[-1] == rows_z else (0, rows_z)
    chunks = len(cuts) - 1

    fields, edges, inner, pots = prepare(phi, pot, cuts)
    halo = []

    def send_halo(c, *before):
        up, down = after(fields[c][-1], *before), after(fields[c][0], *before)
        halo.append((lax.ppermute(up, "gy", shifts("gy", 1)), lax.ppermute(down, "gy", shifts("gy", -1))))

    send_halo(0)
    outer = outer_rows(edges, rows_y)
    req_cols, slot_of, _ = lax.optimization_barrier((req_cols, slot_of, edges))
    kern = kern.reshape(-1, block, block)
    kern_hk = kern_hk.reshape(-1, block, block)
    place = lax.axis_index("gz")
    marks = [place > 0, place < lax.axis_size("gz") - 1]

    def sides(c):
        low = (outer, rows_y) if c == 0 else (inner, (2 * c - 2) * rows_y)
        high = (outer, 0) if c == chunks - 1 else (inner, (2 * c + 1) * rows_y)
        return *low, *high, (c == 0, c == chunks - 1)

    blocks = []

    def phi_columns(c, names):
        if blocks:
            return phi_part(fields[c], groups, names, blocks[1])
        mine, partial, *loaded = phi_part(fields[c], groups, names, kern_hk, kern)
        blocks.extend(loaded)
        return mine, partial

    def all_columns(c, mine, partial, table, cols, halves):
        return action_part(
            mine, partial, *halo[c], *sides(c), pots[c], groups, rows_y, cols, table, blocks[0], halves
        )

    if ring != 4:
        which = block_of_column(slot_of, jnp.arange(listed, dtype=jnp.int32)).reshape(-1)
        table = jnp.concatenate([which, jnp.stack(marks).astype(jnp.int32)])
        hit = req_cols[None, :] == jnp.arange(groups * ring, dtype=jnp.int32)[:, None]
        named = jnp.any(hit, axis=1)
        source = jnp.sum(jnp.where(hit, jnp.arange(listed, dtype=jnp.int32), 0), axis=1)
        parts = []
        for c in range(chunks):
            if c:
                send_halo(c, table)
            _, sums = all_columns(c, *phi_columns(c, which), table, listed, 1)
            spread = jnp.where(named[:, None, None], sums.reshape(listed, -1, block)[source], 0)
            total = lax.psum_scatter(spread, "gx", scatter_dimension=0, tiled=True)
            parts.append([total.reshape(-1, block)])
        flat = finish(parts, (0,), groups, groups, rows_y, rows_z)
        return unflatten(flat, groups, block, rows_y, rows_z // LANES)

    me = lax.axis_index("gx")
    toward = (req_cols // groups - me) % ring
    away = jnp.max(toward)
    ahead = [(i, (i + 1) % ring) for i in range(ring)]
    behind = [(i, (i - 1) % ring) for i in range(ring)]

    half = groups // 2
    column = req_cols % groups
    first = jnp.where(toward == ACROSS, column, (column + half) % groups)
    order = jnp.where(toward == 0, groups + column, first)
    slots = jnp.sum(
        jnp.where(
            jnp.arange(2 * groups, dtype=jnp.int32)[:, None] == order[None, :], jnp.arange(listed, dtype=jnp.int32), 0
        ),
        axis=1,
    )
    which = block_of_column(slot_of, slots).reshape(-1)
    far, near = which[: groups * groups], which[groups * groups :]
    table = jnp.concatenate([far, jnp.stack([*marks, away]).astype(jnp.int32)])
    away = away.reshape(1)
    send_halo(1, far)

    rows, acts, sent, own, right1, left1, right2, left2 = [], [], [], [], [], [], [], []

    def send_first(c, *before):
        mine, partial = phi_columns(c, after(far, *before))
        act, q0, q1 = all_columns(c, mine, partial, after(table, *before), groups, 2)
        rows.append(mine)
        acts.append(act)
        sent.append((q0, q1))
        right1.append(lax.ppermute(q0, "gx", ahead))
        left1.append(lax.ppermute(q1, "gx", behind))

    def send_second(c, *before):
        arrived = lax.optimization_barrier((right1[c], left1[c], *before))
        right1[c], left1[c] = arrived[:2]
        to_right, to_left = send_onward(away, *sent[c], right1[c], left1[c])
        right2.append(lax.ppermute(to_right, "gx", ahead))
        left2.append(lax.ppermute(to_left, "gx", behind))
        own.append(
            local_columns(acts[c], rows[c], groups, after(near, to_right, *right2[:c], *left2[:c]), *blocks, left1[c], right1[c])
        )

    send_first(0)
    for c in range(1, chunks):
        if c + 1 < chunks:
            send_halo(c + 1, sent[c - 1][1])
        send_first(c, *sent[c - 1])
        send_second(c - 1, *sent[c])
    send_second(chunks - 1, own[-1])
    flat = finish(list(zip(own, right2)), (0, 0), half, groups, rows_y, rows_z)
    left2 = lax.optimization_barrier((*left2, flat))
    flat = finish(list(zip(own, left2)), (half, 0), half, groups, rows_y, rows_z, left2[-1])
    return unflatten(flat, groups, block, rows_y, rows_z // LANES)


def solution(mesh):
    placed = (
        P("gx", None, "gy", "gz"),
        P("gx", "gy", "gz"),
        P("gx", None, None, None),
        P("gx", None, None, None),
        P("gx", None),
        P("gx"),
    )
    return jax.shard_map(
        per_device, mesh=mesh, in_specs=placed, out_specs=P("gx", None, "gy", "gz"), check_vma=False
    )
```
